512 devices in a mesh: band: 16 (over x, z_hi, core), pw: 32 (over y, z_lo).
Axes of the slice: x: 4, y: 4, z: 16 (z_hi: 2, z_lo: 8; z = z_hi * 8 + z_lo), core: 2. Of those that a mesh axis runs over, the one named last changes fastest.
Arguments:
- band_coeffs: bfloat16 [16, 2, 4096, 256], P('band', None, 'pw'), may hold values from -6 to 6
- potential: bfloat16 [32, 512, 512], P('pw'), may hold values from -6 to 6
- stick_list: int32 [4096, 2], replicated, may hold values from 1 to 255, as said below
Outputs:
- applied: bfloat16 [16, 2, 4096, 256], P('band', None, 'pw')
- correlation: float32 [2, 16, 16], P(None, None, 'band')
The draws below stay inside these ranges and needn't reach their ends.
Inputs may be any that keep to these rules, and one draw needn't show every extreme that they name: `stick_list`: the rows are distinct box columns (x, y), each with (x - 128)^2 + (y - 128)^2 < 128^2.
All inputs are finite; a program needn't handle non-finite values.
Results may differ from the reference program's by a relative error of at most 0.019.
Values may be sent and summed in bfloat16 or wider, within the bound.
A program may use at most 64 MiB of HBM per device.

```python
import math
import jax
import jax.numpy as jnp
from jax import lax

K = 256
NG = 512
BANDS = 16
STICKS = 4096
SLAB = 32


def draw_stick_list(key, part):
    shuffled = jax.random.permutation(key, K * K).astype(jnp.int32)
    row_a = shuffled // K
    row_b = shuffled % K
    middle = K // 2
    radial = (row_a - middle) * (row_a - middle) + (row_b - middle) * (row_b - middle)
    outside = (radial >= middle * middle).astype(jnp.int32)
    chosen = shuffled[jnp.argsort(outside, stable=True)][:STICKS]
    return jnp.stack([chosen // K, chosen % K], axis=1).astype(jnp.int32)


def block_levels(key, extent, shards, smallest, largest):
    gain = 1.0
    for position, parts in shards:
        heights = jax.random.uniform(jax.random.fold_in(jax.random.fold_in(key, 6), position), (parts,), jnp.float32, smallest / len(shards), largest / len(shards))
        gain = gain * jnp.repeat(jnp.exp(heights), extent[position] // parts).reshape((-1,) + (1,) * (len(extent) - 1 - position))
    return gain


def bell_draw(rng, extent, spread, limit, shards=(), held_as=jnp.bfloat16):
    result = jax.random.normal(rng, extent, jnp.float32) * spread
    if len(shards) > 0:
        result = block_levels(rng, extent, shards, -0.22, 0.18) * result
    return jnp.clip(result, min=-limit, max=limit).astype(held_as)


def setup_inputs(seed: int = 0) -> dict:
    splits = jax.random.split(jax.random.key(seed), 4)
    return {
        "band_coeffs": bell_draw(splits[0], (BANDS, 2, STICKS, K), 1.0, 6.0, ((0, 16), (2, 32))),
        "potential": bell_draw(splits[1], (SLAB, NG, NG), 1.0, 6.0, ((0, 32),)),
        "stick_list": draw_stick_list(jax.random.fold_in(splits[3], 71), 0),
    }


def phase_table(box_count, grid_count, period, sign_value, factor):
    box_index = jnp.arange(box_count, dtype=jnp.int32) - box_count // 2
    grid_index = jnp.arange(grid_count, dtype=jnp.int32)
    phase_turns = box_index[:, None] * grid_index[None, :] % period
    angles = phase_turns.astype(jnp.float32) * (2.0 * math.pi / period)
    cos_part = (jnp.cos(angles) * factor).astype(jnp.bfloat16)
    sin_part = (sign_value * jnp.sin(angles) * factor).astype(jnp.bfloat16)
    return (cos_part, sin_part)

def complex_apply(pattern, real_in, imag_in, tables):
    cos_part = tables[0].astype(jnp.float32)
    sin_part = tables[1].astype(jnp.float32)
    real_in = real_in.astype(jnp.float32)
    imag_in = imag_in.astype(jnp.float32)
    real_out = jnp.einsum(pattern, real_in, cos_part) - jnp.einsum(pattern, imag_in, sin_part)
    imag_out = jnp.einsum(pattern, real_in, sin_part) + jnp.einsum(pattern, imag_in, cos_part)
    return (real_out, imag_out)

def sphere_mask(row_a, row_b, box_edge):
    middle = box_edge // 2
    z_level = jnp.arange(box_edge, dtype=jnp.int32) - middle
    radial = (row_a - middle) * (row_a - middle) + (row_b - middle) * (row_b - middle)
    inside = radial[:, None] + z_level[None, :] * z_level[None, :] < middle * middle
    return inside.astype(jnp.bfloat16)

def plane_work(real_in, imag_in, potential, cell_codes, box_edge, grid_len):
    leading = real_in.shape[:2]
    box_real = jnp.zeros(leading + (box_edge * box_edge,), jnp.bfloat16).at[:, :, cell_codes].set(real_in)
    box_imag = jnp.zeros(leading + (box_edge * box_edge,), jnp.bfloat16).at[:, :, cell_codes].set(imag_in)
    box_real = box_real.reshape(leading + (box_edge, box_edge))
    box_imag = box_imag.reshape(leading + (box_edge, box_edge))
    inverse = phase_table(box_edge, grid_len, grid_len, 1.0, 1.0 / math.sqrt(box_edge))
    forward = phase_table(box_edge, grid_len, grid_len, -1.0, 1.0 / math.sqrt(grid_len))
    half_real, half_imag = complex_apply('bpaj,jy->bpay', box_real, box_imag, inverse)
    half_real = half_real.astype(jnp.bfloat16)
    half_imag = half_imag.astype(jnp.bfloat16)
    field_real, field_imag = complex_apply('bpay,ax->bpxy', half_real, half_imag, inverse)
    pot_field = potential.astype(jnp.float32)[None]
    prod_real = (pot_field * field_real).astype(jnp.bfloat16)
    prod_imag = (pot_field * field_imag).astype(jnp.bfloat16)
    back_real, back_imag = complex_apply('bpxy,ax->bpay', prod_real, prod_imag, forward)
    back_real = back_real.astype(jnp.bfloat16)
    back_imag = back_imag.astype(jnp.bfloat16)
    cell_real, cell_imag = complex_apply('bpay,jy->bpaj', back_real, back_imag, forward)
    cell_real = jnp.take(cell_real.reshape(leading + (box_edge * box_edge,)), cell_codes, axis=2)
    cell_imag = jnp.take(cell_imag.reshape(leading + (box_edge * box_edge,)), cell_codes, axis=2)
    return (cell_real.astype(jnp.bfloat16), cell_imag.astype(jnp.bfloat16))

def reference(band_coeffs, potential, stick_list):
    row_a = stick_list[:, 0]
    row_b = stick_list[:, 1]
    cell_codes = row_a * K + row_b
    sphere = sphere_mask(row_a, row_b, K)
    masked = band_coeffs * sphere[None, None]
    z_inverse = phase_table(K, SLAB, NG, 1.0, 1.0 / math.sqrt(K))
    z_forward = phase_table(K, SLAB, NG, -1.0, 1.0 / math.sqrt(SLAB))

    def one_band(coeffs):
        plane_real, plane_imag = complex_apply('sk,kz->zs', coeffs[0], coeffs[1], z_inverse)
        plane_real = plane_real.astype(jnp.bfloat16)[None]
        plane_imag = plane_imag.astype(jnp.bfloat16)[None]
        back_real, back_imag = plane_work(plane_real, plane_imag, potential, cell_codes, K, NG)
        out_real, out_imag = complex_apply('zs,kz->sk', back_real[0], back_imag[0], z_forward)
        sphere_f = sphere.astype(jnp.float32)
        return jnp.stack([out_real * sphere_f, out_imag * sphere_f]).astype(jnp.bfloat16)
    applied = lax.map(one_band, masked)
    left_side = masked.astype(jnp.float32)
    right_side = applied.astype(jnp.float32)
    real_part = jnp.einsum('icsk,jcsk->ij', left_side, right_side)
    imag_part = jnp.einsum('isk,jsk->ij', left_side[:, 0], right_side[:, 1]) - jnp.einsum('isk,jsk->ij', left_side[:, 1], right_side[:, 0])
    correlation = jnp.stack([real_part, imag_part]) / math.sqrt(STICKS * K)
    return (applied, correlation.astype(jnp.float32))
```

```python
import functools
import math

import jax
import jax.numpy as jnp
import ml_dtypes
import numpy as np
from jax import lax
from jax.experimental import pallas as pl
from jax.experimental.pallas import tpu as pltpu
from jax.sharding import PartitionSpec as P

MESH = pl.DeviceIdType.MESH
BF = jnp.bfloat16
F32 = jnp.float32
NT = (((1,), (1,)), ((), ()))
TN = (((0,), (0,)), ((), ()))


def phase_table(box_count, grid_count, period, sign_value, factor):
    box_index = np.arange(box_count, dtype=np.int64) - box_count // 2
    grid_index = np.arange(grid_count, dtype=np.int64)
    turns = box_index[:, None] * grid_index[None, :] % period
    angles = turns.astype(np.float64) * (2.0 * math.pi / period)
    cos_part = (np.cos(angles) * factor).astype(np.float32).astype(ml_dtypes.bfloat16)
    sin_part = (sign_value * np.sin(angles) * factor).astype(np.float32).astype(ml_dtypes.bfloat16)
    return cos_part, sin_part


def make_tables(box, grid, slab):
    inv_c, inv_s = phase_table(box, grid, grid, 1.0, 1.0 / math.sqrt(box))
    fwd_c, fwd_s = phase_table(box, grid, grid, -1.0, 1.0 / math.sqrt(grid))
    zi_c, zi_s = phase_table(box, slab, grid, 1.0, 1.0 / math.sqrt(box))
    zf_c, zf_s = phase_table(box, slab, grid, -1.0, 1.0 / math.sqrt(slab))
    z_inv = np.stack(
        [np.concatenate([zi_c.T, -zi_s.T], 1), np.concatenate([zi_s.T, zi_c.T], 1)], 1
    ).reshape(2 * slab, 2 * box)
    z_fwd = np.stack(
        [np.concatenate([zf_c.T, zf_s.T], 1), np.concatenate([-zf_s.T, zf_c.T], 1)], 1
    ).reshape(2 * slab, 2 * box)
    y_inv = np.block([[inv_c, inv_s], [-inv_s, inv_c]])
    x_inv = np.block([[inv_c.T, -inv_s.T], [inv_s.T, inv_c.T]])
    x_fwd = np.block([[fwd_c, -fwd_s], [fwd_s, fwd_c]])
    y_fwd = np.block([[fwd_c, -fwd_s], [fwd_s, fwd_c]])
    assert (x_fwd == y_fwd).all()
    return z_inv, z_fwd, y_inv, x_inv, x_fwd


def kernel(
    sizes,
    coeffs_hbm, pot_hbm, sticks_hbm, z_inv_hbm, z_fwd_hbm, y_inv_hbm, x_inv_hbm, fwd_hbm,
    applied_ref, corr_ref,
    coeffs, pot, sticks, z_inv, z_fwd, y_inv, x_inv, fwd,
    hot_a, hot_b, spread, half, prod,
    send1, gath, send2, recv2, part, parts,
    load_sem, send_sem, recv_sem,
):
    bands, planes, box, grid, own, slab = sizes
    me_b = lax.axis_index("band")
    me_p = lax.axis_index("pw")

    loads = [
        pltpu.make_async_copy(src, dst, load_sem.at[n])
        for n, (src, dst) in enumerate(
            [
                (sticks_hbm, sticks), (coeffs_hbm, coeffs), (z_inv_hbm, z_inv),
                (y_inv_hbm, y_inv), (x_inv_hbm, x_inv), (pot_hbm, pot), (fwd_hbm, fwd), (z_fwd_hbm, z_fwd),
            ]
        )
    ]
    for load in loads:
        load.start()

    core = lax.rem(me_b, 2)
    zhi = lax.rem(me_b // 2, 2)
    x_at = me_b // 4
    xs = bands // 4
    sibling = me_b + 1 - 2 * core
    partner = me_b + 2 - 4 * zhi
    x_peers = [lax.rem(x_at + d, xs) * 4 + lax.rem(me_b, 4) for d in range(1, xs)]

    barrier = pltpu.get_barrier_semaphore()

    def greet(step, carry):
        pl.semaphore_signal(
            barrier, inc=1, device_id={"pw": lax.rem(me_p + step, planes)}, device_id_type=MESH
        )
        return carry

    lax.fori_loop(1, planes, greet, 0)
    for peer in [sibling, partner] + x_peers:
        pl.semaphore_signal(barrier, inc=1, device_id={"band": peer}, device_id_type=MESH)

    loads[0].wait()
    loads[1].wait()
    loads[2].wait()
    own_cols = jnp.transpose(
        jnp.concatenate([sticks[me_p], jnp.zeros((6, own), jnp.int32)], axis=0).astype(F32)
    )
    mid = float(box // 2)
    da = own_cols[:, 0:1] - mid
    db = own_cols[:, 1:2] - mid
    radial = da * da + db * db
    kk = lax.broadcasted_iota(jnp.int32, (own, box), 1).astype(F32) - mid
    inside = radial + kk * kk < mid * mid
    masked = jnp.concatenate(
        [
            jnp.where(inside, coeffs[0, 0].astype(F32), 0.0).astype(BF),
            jnp.where(inside, coeffs[0, 1].astype(F32), 0.0).astype(BF),
        ],
        axis=1,
    )
    zp = lax.dot_general(z_inv[...], masked, NT, preferred_element_type=F32)
    for z in range(slab):
        send1[z] = zp[2 * z : 2 * z + 2, :].astype(BF)
    gath[me_b, me_p] = send1[me_p]

    pl.semaphore_wait(barrier, planes - 1 + 2 + len(x_peers))

    def push1(step, carry):
        peer = lax.rem(me_p + step, planes)
        pltpu.make_async_remote_copy(
            src_ref=send1.at[peer],
            dst_ref=gath.at[me_b, me_p],
            send_sem=send_sem.at[0],
            recv_sem=recv_sem.at[0],
            device_id={"pw": peer},
            device_id_type=MESH,
        ).start()
        return carry

    lax.fori_loop(1, planes, push1, 0)

    level = lax.broadcasted_iota(jnp.int32, (box, own), 0).astype(F32).astype(BF)

    def mark(p, carry):
        at = sticks[p].astype(F32).astype(BF)
        cols = pl.ds(pl.multiple_of(p * own, own), own)
        one = jnp.ones((box, own), BF)
        zero = jnp.zeros((box, own), BF)
        hot_a[:, cols] = jnp.where(level == at[0:1, :], one, zero)
        hot_b[:, cols] = jnp.where(level == at[1:2, :], one, zero)
        return carry

    lax.fori_loop(0, planes, mark, 0)
    loads[3].wait()
    loads[4].wait()
    loads[5].wait()
    loads[6].wait()
    loads[7].wait()

    def arrived(ref, index):
        pltpu.make_async_copy(ref, ref, recv_sem.at[index]).wait()

    def forward(block, band, index, sem):
        pltpu.make_async_remote_copy(
            src_ref=gath.at[block],
            dst_ref=gath.at[block],
            send_sem=send_sem.at[sem],
            recv_sem=recv_sem.at[index],
            device_id={"band": band},
            device_id_type=MESH,
        ).start()

    arrived(gath.at[me_b, pl.ds(0, planes - 1)], 0)

    forward(me_b, partner, 1, 1)
    for peer in x_peers:
        forward(me_b, peer, 2, 1)
    forward(me_b, sibling, 4, 1)

    def place(p, carry):
        at = gath[me_b, p]
        cols = pl.ds(pl.multiple_of(p * own, own), own)
        hot = hot_a[:, cols]
        spread[0:box, cols] = hot * at[0:1, :]
        spread[box : 2 * box, cols] = hot * at[1:2, :]
        return carry

    lax.fori_loop(0, planes, place, 0)
    boxed = lax.dot_general(spread[...], hot_b[...], NT, preferred_element_type=F32).astype(BF)
    boxed = jnp.concatenate([boxed[0:box], boxed[box : 2 * box]], axis=1)

    rows = jnp.dot(boxed, y_inv[...], preferred_element_type=F32).astype(BF)
    half[0:box, :] = rows[:, 0:grid]
    half[box : 2 * box, :] = rows[:, grid : 2 * grid]

    arrived(gath.at[0], 1)
    for peer in x_peers:
        forward(partner, peer, 3, 1)
    forward(partner, sibling, 4, 1)

    for t in range(2 * grid // box):
        tile = slice(t * box, (t + 1) * box)
        lane = slice((t * box) % grid, (t * box) % grid + box)
        field = jnp.dot(x_inv[tile, :], half[...], preferred_element_type=F32)
        prod[tile, :] = (pot[0, lane, :].astype(F32) * field).astype(BF)
    hf = jnp.dot(fwd[...], prod[...], preferred_element_type=F32).astype(BF)
    hf = jnp.concatenate([hf[0:box], hf[box : 2 * box]], axis=1)

    arrived(gath.at[pl.ds(0, len(x_peers))], 2)
    for peer in x_peers:
        forward(peer, sibling, 4, 1)

    cell = lax.dot_general(fwd[...], hf, NT, preferred_element_type=F32).astype(BF)

    arrived(gath.at[pl.ds(0, len(x_peers))], 3)
    for peer in x_peers:
        forward(peer + 2 - 4 * zhi, sibling, 4, 1)

    def read(c, carry):
        width = 2 * own
        cols = pl.ds(pl.multiple_of(c * width, width), width)
        picked = jnp.dot(cell, hot_a[:, cols], preferred_element_type=F32)
        hot = hot_b[:, cols].astype(F32)
        re = jnp.sum(picked[0:box] * hot, axis=0, keepdims=True)
        im = jnp.sum(picked[box : 2 * box] * hot, axis=0, keepdims=True)
        both = jnp.concatenate([re, im], axis=0).astype(BF)
        send2[2 * c] = both[:, 0:own]
        send2[2 * c + 1] = both[:, own : 2 * own]
        return carry

    lax.fori_loop(0, planes // 2, read, 0)
    recv2[me_p] = send2[me_p]

    def push2(step, carry):
        peer = lax.rem(me_p + step, planes)
        pltpu.make_async_remote_copy(
            src_ref=send2.at[peer],
            dst_ref=recv2.at[me_p],
            send_sem=send_sem.at[2],
            recv_sem=recv_sem.at[5],
            device_id={"pw": peer},
            device_id_type=MESH,
        ).start()
        return carry

    lax.fori_loop(1, planes, push2, 0)

    arrived(gath.at[pl.ds(0, bands // 2)], 4)
    scale = math.sqrt(box / slab) / math.sqrt(planes * own * box)
    re_rows = []
    im_rows = []
    back = send2[...].astype(F32)
    back_re = back[:, 0:1, :]
    back_im = back[:, 1:2, :]
    for i in range(bands):
        other = gath[i].astype(F32)
        o_re = other[:, 0:1, :]
        o_im = other[:, 1:2, :]
        re_rows.append(jnp.sum(o_re * back_re + o_im * back_im, axis=0))
        im_rows.append(jnp.sum(o_re * back_im - o_im * back_re, axis=0))
    lanes = jnp.concatenate(re_rows + im_rows, axis=0)
    total = jnp.sum(lanes, axis=1, keepdims=True) * scale
    wide = jnp.concatenate([jnp.broadcast_to(total, (2 * bands, own)), jnp.zeros((own - 2 * bands, own), F32)], axis=0)
    part[0] = jnp.transpose(wide)[0:1, :]
    parts[me_p] = part[0]

    def push3(step, carry):
        peer = lax.rem(me_p + step, planes)
        pltpu.make_async_remote_copy(
            src_ref=part.at[0],
            dst_ref=parts.at[me_p],
            send_sem=send_sem.at[3],
            recv_sem=recv_sem.at[6],
            device_id={"pw": peer},
            device_id_type=MESH,
        ).start()
        return carry

    lax.fori_loop(1, planes, push3, 0)

    arrived(recv2.at[pl.ds(0, planes - 1)], 5)
    got = jnp.concatenate([recv2[z].astype(F32) for z in range(slab)], axis=0).astype(BF)
    out = lax.dot_general(got, z_fwd[...], TN, preferred_element_type=F32)
    applied_ref[0, 0] = jnp.where(inside, out[:, 0:box], 0.0).astype(BF)
    applied_ref[0, 1] = jnp.where(inside, out[:, box : 2 * box], 0.0).astype(BF)

    arrived(parts.at[pl.ds(0, planes - 1)], 6)
    corr_ref[...] = jnp.sum(parts[...], axis=0)

    for sem, ref in (
        (0, send1.at[pl.ds(0, planes - 1)]),
        (1, gath.at[pl.ds(0, bands - 1)]),
        (2, send2.at[pl.ds(0, planes - 1)]),
        (3, parts.at[pl.ds(0, planes - 1)]),
    ):
        pltpu.make_async_copy(ref, ref, send_sem.at[sem]).wait()


def local(band_coeffs, potential, stick_list):
    bands = lax.axis_size("band")
    planes = lax.axis_size("pw")
    own = band_coeffs.shape[2]
    box = band_coeffs.shape[3]
    grid = potential.shape[1]
    slab = potential.shape[0] * planes
    z_inv, z_fwd, y_inv, x_inv, fwd = (jnp.asarray(t) for t in make_tables(box, grid, slab))
    sticks = stick_list.T.reshape(2, planes, own).transpose(1, 0, 2)
    any_space = pl.BlockSpec(memory_space=pl.ANY)
    vmem = pl.BlockSpec(memory_space=pltpu.VMEM)
    applied, corr = pl.pallas_call(
        functools.partial(kernel, (bands, planes, box, grid, own, slab)),
        out_shape=(
            jax.ShapeDtypeStruct(band_coeffs.shape, BF),
            jax.ShapeDtypeStruct((1, own), F32),
        ),
        in_specs=[any_space] * 8,
        out_specs=(vmem, vmem),
        scratch_shapes=[
            pltpu.VMEM(band_coeffs.shape, BF),
            pltpu.VMEM(potential.shape, BF),
            pltpu.VMEM(sticks.shape, jnp.int32),
            pltpu.VMEM(z_inv.shape, BF),
            pltpu.VMEM(z_fwd.shape, BF),
            pltpu.VMEM(y_inv.shape, BF),
            pltpu.VMEM(x_inv.shape, BF),
            pltpu.VMEM(fwd.shape, BF),
            pltpu.VMEM((box, planes * own), BF),
            pltpu.VMEM((box, planes * own), BF),
            pltpu.VMEM((2 * box, planes * own), BF),
            pltpu.VMEM((2 * box, grid), BF),
            pltpu.VMEM((2 * grid, grid), BF),
            pltpu.VMEM((slab, 2, own), BF),
            pltpu.VMEM((bands, planes, 2, own), BF),
            pltpu.VMEM((planes, 2, own), BF),
            pltpu.VMEM((slab, 2, own), BF),
            pltpu.VMEM((1, 1, own), F32),
            pltpu.VMEM((planes, 1, own), F32),
            pltpu.SemaphoreType.DMA((8,)),
            pltpu.SemaphoreType.DMA((4,)),
            pltpu.SemaphoreType.DMA((7,)),
        ],
        compiler_params=pltpu.CompilerParams(
            collective_id=0, has_side_effects=True, vmem_limit_bytes=56 * 1024 * 1024
        ),
        name="local_potential",
    )(band_coeffs, potential, sticks, z_inv, z_fwd, y_inv, x_inv, fwd)
    corr = corr[0, : 2 * bands].reshape(2, bands, 1)
    return applied, corr


def solution(mesh):
    return jax.shard_map(
        local,
        mesh=mesh,
        in_specs=(P("band", None, "pw", None), P("pw", None, None), P()),
        out_specs=(P("band", None, "pw", None), P(None, None, "band")),
        check_vma=False,
    )
```

```python
import functools
import math

import jax
import jax.numpy as jnp
import ml_dtypes
import numpy as np
from jax import lax
from jax.experimental import pallas as pl
from jax.experimental.pallas import tpu as pltpu
from jax.sharding import PartitionSpec as P

MESH = pl.DeviceIdType.MESH
BF = jnp.bfloat16
F32 = jnp.float32
NT = (((1,), (1,)), ((), ()))
TN = (((0,), (0,)), ((), ()))
RUN = 8


def phase_table(box_count, grid_count, period, sign_value, factor):
    box_index = np.arange(box_count, dtype=np.int64) - box_count // 2
    grid_index = np.arange(grid_count, dtype=np.int64)
    turns = box_index[:, None] * grid_index[None, :] % period
    angles = turns.astype(np.float64) * (2.0 * math.pi / period)
    cos_part = (np.cos(angles) * factor).astype(np.float32).astype(ml_dtypes.bfloat16)
    sin_part = (sign_value * np.sin(angles) * factor).astype(np.float32).astype(ml_dtypes.bfloat16)
    return cos_part, sin_part


def make_tables(box, grid, slab):
    inv_c, inv_s = phase_table(box, grid, grid, 1.0, 1.0 / math.sqrt(box))
    fwd_c, fwd_s = phase_table(box, grid, grid, -1.0, 1.0 / math.sqrt(grid))
    zi_c, zi_s = phase_table(box, slab, grid, 1.0, 1.0 / math.sqrt(box))
    zf_c, zf_s = phase_table(box, slab, grid, -1.0, 1.0 / math.sqrt(slab))
    z_inv = np.stack(
        [np.concatenate([zi_c.T, -zi_s.T], 1), np.concatenate([zi_s.T, zi_c.T], 1)], 1
    ).reshape(2 * slab, 2 * box)
    z_fwd = np.stack(
        [np.concatenate([zf_c.T, zf_s.T], 1), np.concatenate([-zf_s.T, zf_c.T], 1)], 1
    ).reshape(2 * slab, 2 * box)
    y_inv = np.block([[inv_c, inv_s], [-inv_s, inv_c]])
    x_inv = np.block([[inv_c.T, -inv_s.T], [inv_s.T, inv_c.T]])
    x_fwd = np.block([[fwd_c, -fwd_s], [fwd_s, fwd_c]])
    y_fwd = np.block([[fwd_c, -fwd_s], [fwd_s, fwd_c]])
    assert (x_fwd == y_fwd).all()
    return z_inv, z_fwd, y_inv, x_inv, x_fwd


def kernel(
    sizes,
    coeffs_hbm, pot_hbm, sticks_hbm, z_inv_hbm, z_fwd_hbm, y_inv_hbm, x_inv_hbm, fwd_hbm,
    applied_ref, corr_ref,
    coeffs, pot, sticks, z_inv, z_fwd, y_inv, x_inv, fwd,
    hot_a, hot_b, half, prod,
    send1, mid1, recv1, send2, mid2, recv2, gath, part1, parts1, part2, parts2,
    load_sem, send_sem, recv_sem,
):
    bands, planes, box, grid, own, slab = sizes
    me_b = lax.axis_index("band")
    me_p = lax.axis_index("pw")
    nz = RUN
    ny = planes // nz
    my_z = lax.rem(me_p, nz)
    my_y = me_p // nz

    core = lax.rem(me_b, 2)
    zhi = lax.rem(me_b // 2, 2)
    xs = bands // 4
    sibling = me_b + 1 - 2 * core
    partner = me_b + 2 - 4 * zhi
    x_peers = [lax.rem(me_b + 4 * d, bands) for d in range(1, xs)]
    z_at = [lax.rem(my_z + d, nz) for d in range(1, nz)]
    y_at = [lax.rem(my_y + d, ny) for d in range(1, ny)]
    z_peers = [my_y * nz + z for z in z_at]
    y_peers = [y * nz + my_z for y in y_at]

    barrier = pltpu.get_barrier_semaphore()
    for peer in z_peers + y_peers:
        pl.semaphore_signal(barrier, inc=1, device_id={"pw": peer}, device_id_type=MESH)
    for peer in [partner] + x_peers + [sibling]:
        pl.semaphore_signal(barrier, inc=1, device_id={"band": peer}, device_id_type=MESH)

    loads = [
        pltpu.make_async_copy(src, dst, load_sem.at[n])
        for n, (src, dst) in enumerate(
            [
                (sticks_hbm, sticks), (coeffs_hbm, coeffs), (z_inv_hbm, z_inv),
                (y_inv_hbm, y_inv), (x_inv_hbm, x_inv), (pot_hbm, pot), (fwd_hbm, fwd), (z_fwd_hbm, z_fwd),
            ]
        )
    ]
    for load in loads[:3]:
        load.start()

    def send(src, dst, out, into, where):
        pltpu.make_async_remote_copy(
            src_ref=src,
            dst_ref=dst,
            send_sem=send_sem.at[out],
            recv_sem=recv_sem.at[into],
            device_id=where,
            device_id_type=MESH,
        ).start()

    def arrived(ref, index):
        pltpu.make_async_copy(ref, ref, recv_sem.at[index]).wait()

    def forward(block, band, into):
        send(gath.at[block], gath.at[block], 0, into, {"band": band})

    loads[0].wait()
    own_cols = jnp.transpose(
        jnp.concatenate([sticks[me_p], jnp.zeros((6, own), jnp.int32)], axis=0).astype(F32)
    )
    mid = float(box // 2)
    da = own_cols[:, 0:1] - mid
    db = own_cols[:, 1:2] - mid
    radial = da * da + db * db
    kk = lax.broadcasted_iota(jnp.int32, (own, box), 1).astype(F32) - mid
    inside = radial + kk * kk < mid * mid
    loads[1].wait()
    loads[2].wait()
    masked = jnp.concatenate(
        [
            jnp.where(inside, coeffs[0, 0].astype(F32), 0.0).astype(BF),
            jnp.where(inside, coeffs[0, 1].astype(F32), 0.0).astype(BF),
        ],
        axis=1,
    )
    zp = lax.dot_general(z_inv[...], masked, NT, preferred_element_type=F32)
    for z in range(slab):
        send1[z % nz, z // nz] = zp[2 * z : 2 * z + 2, :].astype(BF)
    gath[me_b] = zp.astype(BF)

    pl.semaphore_wait(barrier, nz - 1 + ny - 1 + 2 + len(x_peers))

    for z, peer in zip(z_at, z_peers):
        send(send1.at[z], mid1.at[my_z], 1, 5, {"pw": peer})
    for load in loads[3:]:
        load.start()
    mid1[my_z] = send1[my_z]

    forward(me_b, partner, 1)
    for peer in x_peers:
        forward(me_b, peer, 2)
    forward(me_b, sibling, 4)

    level = lax.broadcasted_iota(jnp.int32, (box, own), 0).astype(F32).astype(BF)

    def mark(p):
        at = sticks[p].astype(F32).astype(BF)
        cols = slice(p * own, (p + 1) * own)
        one = jnp.ones((box, own), BF)
        zero = jnp.zeros((box, own), BF)
        hot_a[:, cols] = jnp.where(level == at[0:1, :], one, zero)
        hot_b[:, cols] = jnp.where(level == at[1:2, :], one, zero)

    for p in range(planes // 2):
        mark(p)

    arrived(mid1.at[pl.ds(0, nz - 1)], 5)
    for y, peer in zip(y_at, y_peers):
        send(mid1.at[:, y], recv1.at[my_y], 2, 6, {"pw": peer})
    recv1[my_y] = mid1[:, my_y]

    for p in range(planes // 2, planes):
        mark(p)
    for load in loads[3:]:
        load.wait()
    arrived(recv1.at[pl.ds(0, ny - 1)], 6)

    re_cols = []
    im_cols = []
    for p in range(planes):
        at = recv1[p // nz, p % nz]
        hot = hot_a[:, p * own : (p + 1) * own]
        re_cols.append(hot * at[0:1, :])
        im_cols.append(hot * at[1:2, :])
    spread = jnp.concatenate(
        [jnp.concatenate(re_cols, axis=1), jnp.concatenate(im_cols, axis=1)], axis=0
    )
    boxed = lax.dot_general(spread, hot_b[...], NT, preferred_element_type=F32).astype(BF)
    boxed = jnp.concatenate([boxed[0:box], boxed[box : 2 * box]], axis=1)

    rows = jnp.dot(boxed, y_inv[...], preferred_element_type=F32).astype(BF)
    half[0:box, :] = rows[:, 0:grid]
    half[box : 2 * box, :] = rows[:, grid : 2 * grid]

    for t in range(2 * grid // box):
        tile = slice(t * box, (t + 1) * box)
        lane = slice((t * box) % grid, (t * box) % grid + box)
        field = jnp.dot(x_inv[tile, :], half[...], preferred_element_type=F32)
        prod[tile, :] = (pot[0, lane, :].astype(F32) * field).astype(BF)

    arrived(gath.at[0], 1)
    for peer in x_peers:
        forward(partner, peer, 3)
    forward(partner, sibling, 4)

    hf = jnp.dot(fwd[...], prod[...], preferred_element_type=F32).astype(BF)
    hf = jnp.concatenate([hf[0:box], hf[box : 2 * box]], axis=1)
    cell = lax.dot_general(fwd[...], hf, NT, preferred_element_type=F32).astype(BF)

    width = 2 * own
    for c in range(planes // 2):
        cols = slice(c * width, (c + 1) * width)
        picked = jnp.dot(cell, hot_a[:, cols], preferred_element_type=F32)
        hot = hot_b[:, cols].astype(F32)
        re = jnp.sum(picked[0:box] * hot, axis=0, keepdims=True)
        im = jnp.sum(picked[box : 2 * box] * hot, axis=0, keepdims=True)
        both = jnp.concatenate([re, im], axis=0).astype(BF)
        for q in range(2):
            p = 2 * c + q
            send2[p % nz, p // nz] = both[:, q * own : (q + 1) * own]

    for z, peer in zip(z_at, z_peers):
        send(send2.at[z], mid2.at[my_z], 3, 7, {"pw": peer})
    mid2[my_z] = send2[my_z]

    arrived(gath.at[pl.ds(0, len(x_peers))], 2)
    for peer in x_peers:
        forward(peer, sibling, 4)

    arrived(mid2.at[pl.ds(0, nz - 1)], 7)
    for y, peer in zip(y_at, y_peers):
        send(mid2.at[:, y], recv2.at[my_y], 4, 8, {"pw": peer})
    recv2[my_y] = mid2[:, my_y]

    arrived(gath.at[pl.ds(0, len(x_peers))], 3)
    for peer in x_peers:
        forward(peer + 2 - 4 * zhi, sibling, 4)

    arrived(recv2.at[pl.ds(0, ny - 1)], 8)
    back = jnp.concatenate([recv2[z // nz, z % nz].astype(F32) for z in range(slab)], axis=0)

    even = lax.rem(lax.broadcasted_iota(jnp.int32, (2 * slab, own), 0), 2) == 0
    turned = jnp.where(
        even, pltpu.roll(back, 2 * slab - 1, axis=0), -pltpu.roll(back, 1, axis=0)
    )
    arrived(gath.at[pl.ds(0, bands // 2)], 4)
    scale = math.sqrt(box / slab) / math.sqrt(planes * own * box)
    re_rows = []
    im_rows = []
    for i in range(bands):
        other = gath[i].astype(F32)
        re_rows.append(jnp.sum(other * back, axis=0, keepdims=True))
        im_rows.append(jnp.sum(other * turned, axis=0, keepdims=True))
    lanes = jnp.concatenate(re_rows + im_rows, axis=0)
    total = jnp.sum(lanes, axis=1, keepdims=True) * scale
    wide = jnp.concatenate(
        [jnp.broadcast_to(total, (2 * bands, own)), jnp.zeros((own - 2 * bands, own), F32)], axis=0
    )
    part1[...] = jnp.transpose(wide)[0:1, :]
    for peer in z_peers:
        send(part1, parts1.at[my_z], 5, 9, {"pw": peer})
    parts1[my_z] = part1[...]

    out = lax.dot_general(back.astype(BF), z_fwd[...], TN, preferred_element_type=F32)
    applied_ref[0, 0] = jnp.where(inside, out[:, 0:box], 0.0).astype(BF)
    applied_ref[0, 1] = jnp.where(inside, out[:, box : 2 * box], 0.0).astype(BF)

    arrived(parts1.at[pl.ds(0, nz - 1)], 9)
    part2[...] = jnp.sum(parts1[...], axis=0)
    for peer in y_peers:
        send(part2, parts2.at[my_y], 6, 10, {"pw": peer})
    parts2[my_y] = part2[...]
    arrived(parts2.at[pl.ds(0, ny - 1)], 10)
    summed = jnp.sum(parts2[...], axis=0)
    corr_ref[0] = summed[:, 0:bands]
    corr_ref[1] = summed[:, bands : 2 * bands]

    for sem, ref in (
        (0, gath.at[pl.ds(0, bands - 1)]),
        (1, mid1.at[pl.ds(0, nz - 1)]),
        (2, recv1.at[pl.ds(0, ny - 1)]),
        (3, mid2.at[pl.ds(0, nz - 1)]),
        (4, recv2.at[pl.ds(0, ny - 1)]),
        (5, parts1.at[pl.ds(0, nz - 1)]),
        (6, parts2.at[pl.ds(0, ny - 1)]),
    ):
        pltpu.make_async_copy(ref, ref, send_sem.at[sem]).wait()


def local(band_coeffs, potential, stick_list):
    bands = lax.axis_size("band")
    planes = lax.axis_size("pw")
    own = band_coeffs.shape[2]
    box = band_coeffs.shape[3]
    grid = potential.shape[1]
    slab = potential.shape[0] * planes
    z_inv, z_fwd, y_inv, x_inv, fwd = (jnp.asarray(t) for t in make_tables(box, grid, slab))
    sticks = stick_list.T.reshape(2, planes, own).transpose(1, 0, 2)
    any_space = pl.BlockSpec(memory_space=pl.ANY)
    vmem = pl.BlockSpec(memory_space=pltpu.VMEM)
    nz = RUN
    ny = planes // nz
    applied, corr = pl.pallas_call(
        functools.partial(kernel, (bands, planes, box, grid, own, slab)),
        out_shape=(
            jax.ShapeDtypeStruct(band_coeffs.shape, BF),
            jax.ShapeDtypeStruct((2, 1, bands), F32),
        ),
        in_specs=[any_space] * 8,
        out_specs=(vmem, vmem),
        scratch_shapes=[
            pltpu.VMEM(band_coeffs.shape, BF),
            pltpu.VMEM(potential.shape, BF),
            pltpu.VMEM(sticks.shape, jnp.int32),
            pltpu.VMEM(z_inv.shape, BF),
            pltpu.VMEM(z_fwd.shape, BF),
            pltpu.VMEM(y_inv.shape, BF),
            pltpu.VMEM(x_inv.shape, BF),
            pltpu.VMEM(fwd.shape, BF),
            pltpu.VMEM((box, planes * own), BF),
            pltpu.VMEM((box, planes * own), BF),
            pltpu.VMEM((2 * box, grid), BF),
            pltpu.VMEM((2 * grid, grid), BF),
            pltpu.VMEM((nz, ny, 2, own), BF),
            pltpu.VMEM((nz, ny, 2, own), BF),
            pltpu.VMEM((ny, nz, 2, own), BF),
            pltpu.VMEM((nz, ny, 2, own), BF),
            pltpu.VMEM((nz, ny, 2, own), BF),
            pltpu.VMEM((ny, nz, 2, own), BF),
            pltpu.VMEM((bands, 2 * slab, own), BF),
            pltpu.VMEM((1, own), F32),
            pltpu.VMEM((nz, 1, own), F32),
            pltpu.VMEM((1, own), F32),
            pltpu.VMEM((ny, 1, own), F32),
            pltpu.SemaphoreType.DMA((8,)),
            pltpu.SemaphoreType.DMA((7,)),
            pltpu.SemaphoreType.DMA((11,)),
        ],
        compiler_params=pltpu.CompilerParams(
            collective_id=0, has_side_effects=True, vmem_limit_bytes=56 * 1024 * 1024
        ),
        name="local_potential",
    )(band_coeffs, potential, sticks, z_inv, z_fwd, y_inv, x_inv, fwd)
    return applied, corr.transpose(0, 2, 1)


def solution(mesh):
    return jax.shard_map(
        local,
        mesh=mesh,
        in_specs=(P("band", None, "pw", None), P("pw", None, None), P()),
        out_specs=(P("band", None, "pw", None), P(None, None, "band")),
        check_vma=False,
    )
```

```python
import functools
import math

import jax
import jax.numpy as jnp
import ml_dtypes
import numpy as np
from jax import lax
from jax.experimental import pallas as pl
from jax.experimental.pallas import tpu as pltpu
from jax.sharding import PartitionSpec as P

MESH = pl.DeviceIdType.MESH
BF = jnp.bfloat16
F32 = jnp.float32
NT = (((1,), (1,)), ((), ()))
TN = (((0,), (0,)), ((), ()))


def phase_table(box_count, grid_count, period, sign_value, factor):
    box_index = np.arange(box_count, dtype=np.int64) - box_count // 2
    grid_index = np.arange(grid_count, dtype=np.int64)
    turns = box_index[:, None] * grid_index[None, :] % period
    angles = turns.astype(np.float64) * (2.0 * math.pi / period)
    cos_part = (np.cos(angles) * factor).astype(np.float32).astype(ml_dtypes.bfloat16)
    sin_part = (sign_value * np.sin(angles) * factor).astype(np.float32).astype(ml_dtypes.bfloat16)
    return cos_part, sin_part


def make_tables(box, grid, slab):
    inv_c, inv_s = phase_table(box, grid, grid, 1.0, 1.0 / math.sqrt(box))
    fwd_c, fwd_s = phase_table(box, grid, grid, -1.0, 1.0 / math.sqrt(grid))
    zi_c, zi_s = phase_table(box, slab, grid, 1.0, 1.0 / math.sqrt(box))
    zf_c, zf_s = phase_table(box, slab, grid, -1.0, 1.0 / math.sqrt(slab))
    z_inv = np.stack(
        [np.concatenate([zi_c.T, -zi_s.T], 1), np.concatenate([zi_s.T, zi_c.T], 1)], 1
    ).reshape(2 * slab, 2 * box)
    z_fwd = np.stack(
        [np.concatenate([zf_c.T, zf_s.T], 1), np.concatenate([-zf_s.T, zf_c.T], 1)], 1
    ).reshape(2 * slab, 2 * box)
    y_inv = np.block([[inv_c, inv_s], [-inv_s, inv_c]])
    x_inv = np.block([[inv_c.T, -inv_s.T], [inv_s.T, inv_c.T]])
    x_fwd = np.block([[fwd_c, -fwd_s], [fwd_s, fwd_c]])
    y_fwd = np.block([[fwd_c, -fwd_s], [fwd_s, fwd_c]])
    assert (x_fwd == y_fwd).all()
    return z_inv, z_fwd, y_inv, x_inv, x_fwd


def kernel(
    sizes,
    coeffs_hbm, pot_hbm, sticks_hbm, z_inv_hbm, z_fwd_hbm, y_inv_hbm, x_inv_hbm, fwd_hbm,
    applied_ref, corr_ref,
    coeffs, pot, sticks, z_inv, z_fwd, y_inv, x_inv, fwd,
    hot_a, hot_b, half, prod,
    send1, recv1, send2, recv2, gath, part, parts,
    load_sem, send_sem, recv_sem,
):
    bands, planes, box, grid, own, slab = sizes
    me_b = lax.axis_index("band")
    me_p = lax.axis_index("pw")
    core = lax.rem(me_b, 2)
    zhi = lax.rem(me_b // 2, 2)
    xs = bands // 4
    sibling = me_b + 1 - 2 * core
    partner = me_b + 2 - 4 * zhi
    x_peers = [lax.rem(me_b + 4 * d, bands) for d in range(1, xs)]

    barrier = pltpu.get_barrier_semaphore()

    def greet(step, carry):
        pl.semaphore_signal(
            barrier, inc=1, device_id={"pw": lax.rem(me_p + step, planes)}, device_id_type=MESH
        )
        return carry

    lax.fori_loop(1, planes, greet, 0)
    for peer in [partner] + x_peers + [sibling]:
        pl.semaphore_signal(barrier, inc=1, device_id={"band": peer}, device_id_type=MESH)

    loads = [
        pltpu.make_async_copy(src, dst, load_sem.at[n])
        for n, (src, dst) in enumerate(
            [
                (sticks_hbm, sticks), (coeffs_hbm, coeffs), (z_inv_hbm, z_inv),
                (y_inv_hbm, y_inv), (x_inv_hbm, x_inv), (pot_hbm, pot), (fwd_hbm, fwd), (z_fwd_hbm, z_fwd),
            ]
        )
    ]
    for load in loads[:3]:
        load.start()

    def send(src, dst, out, into, where):
        pltpu.make_async_remote_copy(
            src_ref=src,
            dst_ref=dst,
            send_sem=send_sem.at[out],
            recv_sem=recv_sem.at[into],
            device_id=where,
            device_id_type=MESH,
        ).start()

    def arrived(ref, index):
        pltpu.make_async_copy(ref, ref, recv_sem.at[index]).wait()

    def forward(block, band, into):
        send(gath.at[block], gath.at[block], 0, into, {"band": band})

    loads[0].wait()
    own_cols = jnp.transpose(
        jnp.concatenate([sticks[me_p], jnp.zeros((6, own), jnp.int32)], axis=0).astype(F32)
    )
    mid = float(box // 2)
    da = own_cols[:, 0:1] - mid
    db = own_cols[:, 1:2] - mid
    radial = da * da + db * db
    kk = lax.broadcasted_iota(jnp.int32, (own, box), 1).astype(F32) - mid
    inside = radial + kk * kk < mid * mid
    loads[1].wait()
    loads[2].wait()
    masked = jnp.concatenate(
        [
            jnp.where(inside, coeffs[0, 0].astype(F32), 0.0).astype(BF),
            jnp.where(inside, coeffs[0, 1].astype(F32), 0.0).astype(BF),
        ],
        axis=1,
    )
    zp = lax.dot_general(z_inv[...], masked, NT, preferred_element_type=F32)
    for z in range(slab):
        send1[z] = zp[2 * z : 2 * z + 2, :].astype(BF)
    gath[me_b] = zp.astype(BF)

    pl.semaphore_wait(barrier, planes - 1 + 2 + len(x_peers))

    def exchange(pick, dst, out, into):
        def push(step, carry):
            peer = lax.rem(me_p + step, planes)
            send(pick(peer), dst.at[me_p], out, into, {"pw": peer})
            return carry

        lax.fori_loop(1, planes, push, 0)

    exchange(lambda peer: send1.at[peer], recv1, 1, 5)
    for load in loads[3:]:
        load.start()
    recv1[me_p] = send1[me_p]

    forward(me_b, partner, 1)
    for peer in x_peers:
        forward(me_b, peer, 2)
    forward(me_b, sibling, 4)

    level = lax.broadcasted_iota(jnp.int32, (box, own), 0).astype(F32).astype(BF)

    def mark(p):
        at = sticks[p].astype(F32).astype(BF)
        cols = slice(p * own, (p + 1) * own)
        one = jnp.ones((box, own), BF)
        zero = jnp.zeros((box, own), BF)
        hot_a[:, cols] = jnp.where(level == at[0:1, :], one, zero)
        hot_b[:, cols] = jnp.where(level == at[1:2, :], one, zero)

    for p in range(planes):
        mark(p)
    for load in loads[3:]:
        load.wait()
    arrived(recv1.at[pl.ds(0, planes - 1)], 5)

    arrived(gath.at[0], 1)
    for peer in x_peers:
        forward(partner, peer, 3)
    forward(partner, sibling, 4)
    arrived(gath.at[pl.ds(0, len(x_peers))], 2)
    for peer in x_peers:
        forward(peer, sibling, 4)

    re_cols = []
    im_cols = []
    for p in range(planes):
        at = recv1[p]
        hot = hot_a[:, p * own : (p + 1) * own]
        re_cols.append(hot * at[0:1, :])
        im_cols.append(hot * at[1:2, :])
    spread = jnp.concatenate(
        [jnp.concatenate(re_cols, axis=1), jnp.concatenate(im_cols, axis=1)], axis=0
    )
    boxed = lax.dot_general(spread, hot_b[...], NT, preferred_element_type=F32).astype(BF)
    boxed = jnp.concatenate([boxed[0:box], boxed[box : 2 * box]], axis=1)

    rows = jnp.dot(boxed, y_inv[...], preferred_element_type=F32).astype(BF)
    half[0:box, :] = rows[:, 0:grid]
    half[box : 2 * box, :] = rows[:, grid : 2 * grid]

    for t in range(2 * grid // box):
        tile = slice(t * box, (t + 1) * box)
        lane = slice((t * box) % grid, (t * box) % grid + box)
        field = jnp.dot(x_inv[tile, :], half[...], preferred_element_type=F32)
        prod[tile, :] = (pot[0, lane, :].astype(F32) * field).astype(BF)

    hf = jnp.dot(fwd[...], prod[...], preferred_element_type=F32).astype(BF)
    hf = jnp.concatenate([hf[0:box], hf[box : 2 * box]], axis=1)
    cell = lax.dot_general(fwd[...], hf, NT, preferred_element_type=F32).astype(BF)

    width = 2 * own
    for c in range(planes // 2):
        cols = slice(c * width, (c + 1) * width)
        picked = jnp.dot(cell, hot_a[:, cols], preferred_element_type=F32)
        hot = hot_b[:, cols].astype(F32)
        re = jnp.sum(picked[0:box] * hot, axis=0, keepdims=True)
        im = jnp.sum(picked[box : 2 * box] * hot, axis=0, keepdims=True)
        both = jnp.concatenate([re, im], axis=0).astype(BF)
        for q in range(2):
            p = 2 * c + q
            send2[p] = both[:, q * own : (q + 1) * own]

    exchange(lambda peer: send2.at[peer], recv2, 2, 6)
    recv2[me_p] = send2[me_p]

    arrived(gath.at[pl.ds(0, len(x_peers))], 3)
    for peer in x_peers:
        forward(peer + 2 - 4 * zhi, sibling, 4)

    arrived(recv2.at[pl.ds(0, planes - 1)], 6)
    back = jnp.concatenate([recv2[z].astype(F32) for z in range(slab)], axis=0)

    even = lax.rem(lax.broadcasted_iota(jnp.int32, (2 * slab, own), 0), 2) == 0
    turned = jnp.where(
        even, pltpu.roll(back, 2 * slab - 1, axis=0), -pltpu.roll(back, 1, axis=0)
    )
    arrived(gath.at[pl.ds(0, bands // 2)], 4)
    scale = math.sqrt(box / slab) / math.sqrt(planes * own * box)
    re_rows = []
    im_rows = []
    for i in range(bands):
        other = gath[i].astype(F32)
        re_rows.append(jnp.sum(other * back, axis=0, keepdims=True))
        im_rows.append(jnp.sum(other * turned, axis=0, keepdims=True))
    lanes = jnp.concatenate(re_rows + im_rows, axis=0)
    total = jnp.sum(lanes, axis=1, keepdims=True) * scale
    wide = jnp.concatenate(
        [jnp.broadcast_to(total, (2 * bands, own)), jnp.zeros((own - 2 * bands, own), F32)], axis=0
    )
    part[...] = jnp.transpose(wide)[0:1, :]
    exchange(lambda peer: part, parts, 3, 7)
    parts[me_p] = part[...]

    out = lax.dot_general(back.astype(BF), z_fwd[...], TN, preferred_element_type=F32)
    applied_ref[0, 0] = jnp.where(inside, out[:, 0:box], 0.0).astype(BF)
    applied_ref[0, 1] = jnp.where(inside, out[:, box : 2 * box], 0.0).astype(BF)

    arrived(parts.at[pl.ds(0, planes - 1)], 7)
    summed = jnp.sum(parts[...], axis=0)
    corr_ref[0] = summed[:, 0:bands]
    corr_ref[1] = summed[:, bands : 2 * bands]

    for sem, ref in (
        (0, gath.at[pl.ds(0, bands - 1)]),
        (1, recv1.at[pl.ds(0, planes - 1)]),
        (2, recv2.at[pl.ds(0, planes - 1)]),
        (3, parts.at[pl.ds(0, planes - 1)]),
    ):
        pltpu.make_async_copy(ref, ref, send_sem.at[sem]).wait()


def local(band_coeffs, potential, stick_list):
    bands = lax.axis_size("band")
    planes = lax.axis_size("pw")
    own = band_coeffs.shape[2]
    box = band_coeffs.shape[3]
    grid = potential.shape[1]
    slab = potential.shape[0] * planes
    z_inv, z_fwd, y_inv, x_inv, fwd = (jnp.asarray(t) for t in make_tables(box, grid, slab))
    sticks = stick_list.T.reshape(2, planes, own).transpose(1, 0, 2)
    any_space = pl.BlockSpec(memory_space=pl.ANY)
    vmem = pl.BlockSpec(memory_space=pltpu.VMEM)
    applied, corr = pl.pallas_call(
        functools.partial(kernel, (bands, planes, box, grid, own, slab)),
        out_shape=(
            jax.ShapeDtypeStruct(band_coeffs.shape, BF),
            jax.ShapeDtypeStruct((2, 1, bands), F32),
        ),
        in_specs=[any_space] * 8,
        out_specs=(vmem, vmem),
        scratch_shapes=[
            pltpu.VMEM(band_coeffs.shape, BF),
            pltpu.VMEM(potential.shape, BF),
            pltpu.VMEM(sticks.shape, jnp.int32),
            pltpu.VMEM(z_inv.shape, BF),
            pltpu.VMEM(z_fwd.shape, BF),
            pltpu.VMEM(y_inv.shape, BF),
            pltpu.VMEM(x_inv.shape, BF),
            pltpu.VMEM(fwd.shape, BF),
            pltpu.VMEM((box, planes * own), BF),
            pltpu.VMEM((box, planes * own), BF),
            pltpu.VMEM((2 * box, grid), BF),
            pltpu.VMEM((2 * grid, grid), BF),
            pltpu.VMEM((slab, 2, own), BF),
            pltpu.VMEM((planes, 2, own), BF),
            pltpu.VMEM((planes, 2, own), BF),
            pltpu.VMEM((slab, 2, own), BF),
            pltpu.VMEM((bands, 2 * slab, own), BF),
            pltpu.VMEM((1, own), F32),
            pltpu.VMEM((planes, 1, own), F32),
            pltpu.SemaphoreType.DMA((8,)),
            pltpu.SemaphoreType.DMA((4,)),
            pltpu.SemaphoreType.DMA((8,)),
        ],
        compiler_params=pltpu.CompilerParams(
            collective_id=0, has_side_effects=True, vmem_limit_bytes=56 * 1024 * 1024
        ),
        name="local_potential",
    )(band_coeffs, potential, sticks, z_inv, z_fwd, y_inv, x_inv, fwd)
    return applied, corr.transpose(0, 2, 1)


def solution(mesh):
    return jax.shard_map(
        local,
        mesh=mesh,
        in_specs=(P("band", None, "pw", None), P("pw", None, None), P()),
        out_specs=(P("band", None, "pw", None), P(None, None, "band")),
        check_vma=False,
    )
```

```python
import functools
import math

import jax
import jax.numpy as jnp
import ml_dtypes
import numpy as np
from jax import lax
from jax.experimental import pallas as pl
from jax.experimental.pallas import tpu as pltpu
from jax.sharding import PartitionSpec as P

MESH = pl.DeviceIdType.MESH
BF = jnp.bfloat16
F32 = jnp.float32
NT = (((1,), (1,)), ((), ()))
TN = (((0,), (0,)), ((), ()))
RUN = 8


def phase_table(box_count, grid_count, period, sign_value, factor):
    box_index = np.arange(box_count, dtype=np.int64) - box_count // 2
    grid_index = np.arange(grid_count, dtype=np.int64)
    turns = box_index[:, None] * grid_index[None, :] % period
    angles = turns.astype(np.float64) * (2.0 * math.pi / period)
    cos_part = (np.cos(angles) * factor).astype(np.float32).astype(ml_dtypes.bfloat16)
    sin_part = (sign_value * np.sin(angles) * factor).astype(np.float32).astype(ml_dtypes.bfloat16)
    return cos_part, sin_part


def make_tables(box, grid, slab):
    inv_c, inv_s = phase_table(box, grid, grid, 1.0, 1.0 / math.sqrt(box))
    fwd_c, fwd_s = phase_table(box, grid, grid, -1.0, 1.0 / math.sqrt(grid))
    zi_c, zi_s = phase_table(box, slab, grid, 1.0, 1.0 / math.sqrt(box))
    zf_c, zf_s = phase_table(box, slab, grid, -1.0, 1.0 / math.sqrt(slab))
    z_inv = np.stack(
        [np.concatenate([zi_c.T, -zi_s.T], 1), np.concatenate([zi_s.T, zi_c.T], 1)], 1
    ).reshape(2 * slab, 2 * box)
    z_fwd = np.stack(
        [np.concatenate([zf_c.T, zf_s.T], 1), np.concatenate([-zf_s.T, zf_c.T], 1)], 1
    ).reshape(2 * slab, 2 * box)
    y_inv = np.block([[inv_c, inv_s], [-inv_s, inv_c]])
    x_inv = np.block([[inv_c.T, -inv_s.T], [inv_s.T, inv_c.T]])
    x_fwd = np.block([[fwd_c, -fwd_s], [fwd_s, fwd_c]])
    y_fwd = np.block([[fwd_c, -fwd_s], [fwd_s, fwd_c]])
    assert (x_fwd == y_fwd).all()
    return z_inv, z_fwd, y_inv, x_inv, x_fwd


def kernel(
    sizes,
    coeffs_hbm, pot_hbm, sticks_hbm, z_inv_hbm, z_fwd_hbm, y_inv_hbm, x_inv_hbm, fwd_hbm,
    applied_ref, corr_ref,
    coeffs, pot, sticks, z_inv, z_fwd, y_inv, x_inv, fwd,
    hot_a, hot_b, half, prod,
    send1, recv1, send2, recv2, gath, part, parts,
    load_sem, send_sem, recv_sem,
):
    bands, planes, box, grid, own, slab = sizes
    me_b = lax.axis_index("band")
    me_p = lax.axis_index("pw")
    nz = RUN
    ny = planes // nz
    my_z = lax.rem(me_p, nz)
    my_y = me_p // nz
    low = 1 - my_z // (nz // 2)
    y_far = sorted(range(ny), key=lambda d: -min(d, ny - d))

    def place_of(dy, z):
        return lax.rem(my_y + dy, ny) * nz + z

    far = []
    for k in range(nz - 1):
        down = nz - 1 - k - (k + my_z) // (nz - 1)
        up = k + (k + nz - my_z) // nz
        far += [place_of(dy, low * down + (1 - low) * up) for dy in y_far]
    far += [place_of(dy, my_z) for dy in y_far if dy]
    core = lax.rem(me_b, 2)
    zhi = lax.rem(me_b // 2, 2)
    xs = bands // 4
    sibling = me_b + 1 - 2 * core
    partner = me_b + 2 - 4 * zhi
    x_peers = [lax.rem(me_b + 4 * d, bands) for d in range(1, xs)]

    barrier = pltpu.get_barrier_semaphore()

    def greet(step, carry):
        pl.semaphore_signal(
            barrier, inc=1, device_id={"pw": lax.rem(me_p + step, planes)}, device_id_type=MESH
        )
        return carry

    lax.fori_loop(1, planes, greet, 0)
    for peer in [partner] + x_peers + [sibling]:
        pl.semaphore_signal(barrier, inc=1, device_id={"band": peer}, device_id_type=MESH)

    loads = [
        pltpu.make_async_copy(src, dst, load_sem.at[n])
        for n, (src, dst) in enumerate(
            [
                (sticks_hbm, sticks), (coeffs_hbm, coeffs), (z_inv_hbm, z_inv),
                (y_inv_hbm, y_inv), (x_inv_hbm, x_inv), (pot_hbm, pot), (fwd_hbm, fwd), (z_fwd_hbm, z_fwd),
            ]
        )
    ]
    for load in loads[:3]:
        load.start()

    def send(src, dst, out, into, where):
        pltpu.make_async_remote_copy(
            src_ref=src,
            dst_ref=dst,
            send_sem=send_sem.at[out],
            recv_sem=recv_sem.at[into],
            device_id=where,
            device_id_type=MESH,
        ).start()

    def arrived(ref, index):
        pltpu.make_async_copy(ref, ref, recv_sem.at[index]).wait()

    def forward(block, band, into):
        send(gath.at[block], gath.at[block], 0, into, {"band": band})

    loads[0].wait()
    own_cols = jnp.transpose(
        jnp.concatenate([sticks[me_p], jnp.zeros((6, own), jnp.int32)], axis=0).astype(F32)
    )
    mid = float(box // 2)
    da = own_cols[:, 0:1] - mid
    db = own_cols[:, 1:2] - mid
    radial = da * da + db * db
    kk = lax.broadcasted_iota(jnp.int32, (own, box), 1).astype(F32) - mid
    inside = radial + kk * kk < mid * mid
    loads[1].wait()
    loads[2].wait()
    masked = jnp.concatenate(
        [
            jnp.where(inside, coeffs[0, 0].astype(F32), 0.0).astype(BF),
            jnp.where(inside, coeffs[0, 1].astype(F32), 0.0).astype(BF),
        ],
        axis=1,
    )
    zp = lax.dot_general(z_inv[...], masked, NT, preferred_element_type=F32)
    for z in range(slab):
        send1[z] = zp[2 * z : 2 * z + 2, :].astype(BF)
    gath[me_b] = zp.astype(BF)

    pl.semaphore_wait(barrier, planes - 1 + 2 + len(x_peers))

    def exchange(pick, dst, out, into):
        for peer in far:
            send(pick(peer), dst.at[me_p], out, into, {"pw": peer})

    exchange(lambda peer: send1.at[peer], recv1, 1, 5)
    for load in loads[3:]:
        load.start()
    recv1[me_p] = send1[me_p]

    forward(me_b, partner, 1)
    for peer in x_peers:
        forward(me_b, peer, 2)
    forward(me_b, sibling, 4)

    level = lax.broadcasted_iota(jnp.int32, (box, own), 0).astype(F32).astype(BF)

    def mark(p):
        at = sticks[p].astype(F32).astype(BF)
        cols = slice(p * own, (p + 1) * own)
        one = jnp.ones((box, own), BF)
        zero = jnp.zeros((box, own), BF)
        hot_a[:, cols] = jnp.where(level == at[0:1, :], one, zero)
        hot_b[:, cols] = jnp.where(level == at[1:2, :], one, zero)

    for p in range(planes):
        mark(p)
    for load in loads[3:]:
        load.wait()
    arrived(recv1.at[pl.ds(0, planes - 1)], 5)

    re_cols = []
    im_cols = []
    for p in range(planes):
        at = recv1[p]
        hot = hot_a[:, p * own : (p + 1) * own]
        re_cols.append(hot * at[0:1, :])
        im_cols.append(hot * at[1:2, :])
    spread = jnp.concatenate(
        [jnp.concatenate(re_cols, axis=1), jnp.concatenate(im_cols, axis=1)], axis=0
    )
    boxed = lax.dot_general(spread, hot_b[...], NT, preferred_element_type=F32).astype(BF)
    boxed = jnp.concatenate([boxed[0:box], boxed[box : 2 * box]], axis=1)

    rows = jnp.dot(boxed, y_inv[...], preferred_element_type=F32).astype(BF)
    half[0:box, :] = rows[:, 0:grid]
    half[box : 2 * box, :] = rows[:, grid : 2 * grid]

    for t in range(2 * grid // box):
        tile = slice(t * box, (t + 1) * box)
        lane = slice((t * box) % grid, (t * box) % grid + box)
        field = jnp.dot(x_inv[tile, :], half[...], preferred_element_type=F32)
        prod[tile, :] = (pot[0, lane, :].astype(F32) * field).astype(BF)

    hf = jnp.dot(fwd[...], prod[...], preferred_element_type=F32).astype(BF)
    hf = jnp.concatenate([hf[0:box], hf[box : 2 * box]], axis=1)
    arrived(gath.at[0], 1)
    for peer in x_peers:
        forward(partner, peer, 3)
    forward(partner, sibling, 4)
    arrived(gath.at[pl.ds(0, len(x_peers))], 2)
    for peer in x_peers:
        forward(peer, sibling, 4)

    cell = lax.dot_general(fwd[...], hf, NT, preferred_element_type=F32).astype(BF)

    width = 2 * own
    runs = nz // 2
    for k in range(runs):
        run = low * (runs - 1 - k) + (1 - low) * k
        for dy in y_far:
            p = place_of(dy, 2 * run)
            cols = pl.ds(pl.multiple_of(p * own, width), width)
            picked = jnp.dot(cell, hot_a[:, cols], preferred_element_type=F32)
            hot = hot_b[:, cols].astype(F32)
            re = jnp.sum(picked[0:box] * hot, axis=0, keepdims=True)
            im = jnp.sum(picked[box : 2 * box] * hot, axis=0, keepdims=True)
            both = jnp.concatenate([re, im], axis=0).astype(BF)
            for q in range(2):
                send2[p + q] = both[:, q * own : (q + 1) * own]
        for dy in y_far:
            for q in range(2):
                peer = place_of(dy, 2 * run + q)

                def push(peer=peer):
                    send(send2.at[peer], recv2.at[me_p], 2, 6, {"pw": peer})

                if dy:
                    push()
                else:
                    pl.when(peer != me_p)(push)
    recv2[me_p] = send2[me_p]

    arrived(gath.at[pl.ds(0, len(x_peers))], 3)
    for peer in x_peers:
        forward(peer + 2 - 4 * zhi, sibling, 4)

    arrived(recv2.at[pl.ds(0, planes - 1)], 6)
    back = jnp.concatenate([recv2[z].astype(F32) for z in range(slab)], axis=0)

    even = lax.rem(lax.broadcasted_iota(jnp.int32, (2 * slab, own), 0), 2) == 0
    turned = jnp.where(
        even, pltpu.roll(back, 2 * slab - 1, axis=0), -pltpu.roll(back, 1, axis=0)
    )
    arrived(gath.at[pl.ds(0, bands // 2)], 4)
    scale = math.sqrt(box / slab) / math.sqrt(planes * own * box)
    re_rows = []
    im_rows = []
    for i in range(bands):
        other = gath[i].astype(F32)
        re_rows.append(jnp.sum(other * back, axis=0, keepdims=True))
        im_rows.append(jnp.sum(other * turned, axis=0, keepdims=True))
    lanes = jnp.concatenate(re_rows + im_rows, axis=0)
    total = jnp.sum(lanes, axis=1, keepdims=True) * scale
    wide = jnp.concatenate(
        [jnp.broadcast_to(total, (2 * bands, own)), jnp.zeros((own - 2 * bands, own), F32)], axis=0
    )
    part[...] = jnp.transpose(wide)[0:1, :]
    exchange(lambda peer: part, parts, 3, 7)
    parts[me_p] = part[...]

    out = lax.dot_general(back.astype(BF), z_fwd[...], TN, preferred_element_type=F32)
    applied_ref[0, 0] = jnp.where(inside, out[:, 0:box], 0.0).astype(BF)
    applied_ref[0, 1] = jnp.where(inside, out[:, box : 2 * box], 0.0).astype(BF)

    arrived(parts.at[pl.ds(0, planes - 1)], 7)
    summed = jnp.sum(parts[...], axis=0)
    corr_ref[0] = summed[:, 0:bands]
    corr_ref[1] = summed[:, bands : 2 * bands]

    for sem, ref in (
        (0, gath.at[pl.ds(0, bands - 1)]),
        (1, recv1.at[pl.ds(0, planes - 1)]),
        (2, recv2.at[pl.ds(0, planes - 1)]),
        (3, parts.at[pl.ds(0, planes - 1)]),
    ):
        pltpu.make_async_copy(ref, ref, send_sem.at[sem]).wait()


def local(band_coeffs, potential, stick_list):
    bands = lax.axis_size("band")
    planes = lax.axis_size("pw")
    own = band_coeffs.shape[2]
    box = band_coeffs.shape[3]
    grid = potential.shape[1]
    slab = potential.shape[0] * planes
    z_inv, z_fwd, y_inv, x_inv, fwd = (jnp.asarray(t) for t in make_tables(box, grid, slab))
    sticks = stick_list.T.reshape(2, planes, own).transpose(1, 0, 2)
    any_space = pl.BlockSpec(memory_space=pl.ANY)
    vmem = pl.BlockSpec(memory_space=pltpu.VMEM)
    applied, corr = pl.pallas_call(
        functools.partial(kernel, (bands, planes, box, grid, own, slab)),
        out_shape=(
            pltpu.VMEM(band_coeffs.shape, BF),
            pltpu.VMEM((2, 1, bands), F32),
        ),
        in_specs=[any_space] * 8,
        out_specs=(vmem, vmem),
        scratch_shapes=[
            pltpu.VMEM(band_coeffs.shape, BF),
            pltpu.VMEM(potential.shape, BF),
            pltpu.VMEM(sticks.shape, jnp.int32),
            pltpu.VMEM(z_inv.shape, BF),
            pltpu.VMEM(z_fwd.shape, BF),
            pltpu.VMEM(y_inv.shape, BF),
            pltpu.VMEM(x_inv.shape, BF),
            pltpu.VMEM(fwd.shape, BF),
            pltpu.VMEM((box, planes * own), BF),
            pltpu.VMEM((box, planes * own), BF),
            pltpu.VMEM((2 * box, grid), BF),
            pltpu.VMEM((2 * grid, grid), BF),
            pltpu.VMEM((slab, 2, own), BF),
            pltpu.VMEM((planes, 2, own), BF),
            pltpu.VMEM((planes, 2, own), BF),
            pltpu.VMEM((slab, 2, own), BF),
            pltpu.VMEM((bands, 2 * slab, own), BF),
            pltpu.VMEM((1, own), F32),
            pltpu.VMEM((planes, 1, own), F32),
            pltpu.SemaphoreType.DMA((8,)),
            pltpu.SemaphoreType.DMA((4,)),
            pltpu.SemaphoreType.DMA((8,)),
        ],
        compiler_params=pltpu.CompilerParams(
            collective_id=0, has_side_effects=True, vmem_limit_bytes=56 * 1024 * 1024
        ),
        name="local_potential",
    )(band_coeffs, potential, sticks, z_inv, z_fwd, y_inv, x_inv, fwd)
    return applied, corr.transpose(0, 2, 1)


def solution(mesh):
    return jax.shard_map(
        local,
        mesh=mesh,
        in_specs=(P("band", None, "pw", None), P("pw", None, None), P()),
        out_specs=(P("band", None, "pw", None), P(None, None, "band")),
        check_vma=False,
    )
```

```python
import functools
import math

import jax
import jax.numpy as jnp
import ml_dtypes
import numpy as np
from jax import lax
from jax.experimental import pallas as pl
from jax.experimental.pallas import tpu as pltpu
from jax.sharding import PartitionSpec as P

MESH = pl.DeviceIdType.MESH
BF = jnp.bfloat16
F32 = jnp.float32
NT = (((1,), (1,)), ((), ()))
TN = (((0,), (0,)), ((), ()))
RUN = 8


def phase_table(box_count, grid_count, period, sign_value, factor):
    box_index = np.arange(box_count, dtype=np.int64) - box_count // 2
    grid_index = np.arange(grid_count, dtype=np.int64)
    turns = box_index[:, None] * grid_index[None, :] % period
    angles = turns.astype(np.float64) * (2.0 * math.pi / period)
    cos_part = (np.cos(angles) * factor).astype(np.float32).astype(ml_dtypes.bfloat16)
    sin_part = (sign_value * np.sin(angles) * factor).astype(np.float32).astype(ml_dtypes.bfloat16)
    return cos_part, sin_part


def make_tables(box, grid, slab):
    inv_c, inv_s = phase_table(box, grid, grid, 1.0, 1.0 / math.sqrt(box))
    fwd_c, fwd_s = phase_table(box, grid, grid, -1.0, 1.0 / math.sqrt(grid))
    zi_c, zi_s = phase_table(box, slab, grid, 1.0, 1.0 / math.sqrt(box))
    zf_c, zf_s = phase_table(box, slab, grid, -1.0, 1.0 / math.sqrt(slab))
    z_inv = np.stack(
        [np.concatenate([zi_c.T, -zi_s.T], 1), np.concatenate([zi_s.T, zi_c.T], 1)], 1
    ).reshape(2 * slab, 2 * box)
    z_fwd = np.stack(
        [np.concatenate([zf_c.T, zf_s.T], 1), np.concatenate([-zf_s.T, zf_c.T], 1)], 1
    ).reshape(2 * slab, 2 * box)
    y_inv = np.block([[inv_c, inv_s], [-inv_s, inv_c]])
    x_inv = np.block([[inv_c.T, -inv_s.T], [inv_s.T, inv_c.T]])
    x_fwd = np.block([[fwd_c, -fwd_s], [fwd_s, fwd_c]])
    y_fwd = np.block([[fwd_c, -fwd_s], [fwd_s, fwd_c]])
    assert (x_fwd == y_fwd).all()
    return z_inv, z_fwd, y_inv, x_inv, x_fwd


def kernel(
    sizes,
    coeffs_hbm, pot_hbm, sticks_hbm, z_inv_hbm, z_fwd_hbm, y_inv_hbm, x_inv_hbm, fwd_hbm,
    applied_ref, corr_ref,
    coeffs, pot, sticks, z_inv, z_fwd, y_inv, x_inv, fwd,
    hot_a, hot_b, half, prod,
    send1, recv1, send2, recv2, gath, part, parts,
    load_sem, send_sem, recv_sem,
):
    bands, planes, box, grid, own, slab = sizes
    me_b = lax.axis_index("band")
    me_p = lax.axis_index("pw")
    nz = RUN
    ny = planes // nz
    my_z = lax.rem(me_p, nz)
    my_y = me_p // nz
    low = 1 - my_z // (nz // 2)
    y_far = sorted(range(ny), key=lambda d: -min(d, ny - d))

    def place_of(dy, z):
        return lax.rem(my_y + dy, ny) * nz + z

    far = []
    for k in range(nz - 1):
        down = nz - 1 - k - (k + my_z) // (nz - 1)
        up = k + (k + nz - my_z) // nz
        far += [place_of(dy, low * down + (1 - low) * up) for dy in y_far]
    far += [place_of(dy, my_z) for dy in y_far if dy]
    core = lax.rem(me_b, 2)
    zhi = lax.rem(me_b // 2, 2)
    xs = bands // 4
    sibling = me_b + 1 - 2 * core
    partner = me_b + 2 - 4 * zhi
    x_peers = [lax.rem(me_b + 4 * d, bands) for d in range(1, xs)]

    barrier = pltpu.get_barrier_semaphore()

    def greet(step, carry):
        pl.semaphore_signal(
            barrier, inc=1, device_id={"pw": lax.rem(me_p + step, planes)}, device_id_type=MESH
        )
        return carry

    lax.fori_loop(1, planes, greet, 0)

    def hello(peer):
        pl.semaphore_signal(barrier, inc=1, device_id={"band": peer}, device_id_type=MESH)

    for peer in x_peers:
        hello(peer)

    @pl.when(zhi == 0)
    def _():
        hello(partner)

    @pl.when(core == 0)
    def _():
        hello(sibling)

    loads = [
        pltpu.make_async_copy(src, dst, load_sem.at[n])
        for n, (src, dst) in enumerate(
            [
                (sticks_hbm, sticks), (coeffs_hbm, coeffs), (z_inv_hbm, z_inv),
                (y_inv_hbm, y_inv), (x_inv_hbm, x_inv), (pot_hbm, pot), (fwd_hbm, fwd), (z_fwd_hbm, z_fwd),
            ]
        )
    ]
    for load in loads[:3]:
        load.start()

    def send(src, dst, out, into, where):
        pltpu.make_async_remote_copy(
            src_ref=src,
            dst_ref=dst,
            send_sem=send_sem.at[out],
            recv_sem=recv_sem.at[into],
            device_id=where,
            device_id_type=MESH,
        ).start()

    def arrived(ref, index):
        pltpu.make_async_copy(ref, ref, recv_sem.at[index]).wait()

    def forward(block, band, into):
        send(gath.at[block], gath.at[block], 0, into, {"band": band})

    loads[0].wait()
    own_cols = jnp.transpose(
        jnp.concatenate([sticks[me_p], jnp.zeros((6, own), jnp.int32)], axis=0).astype(F32)
    )
    mid = float(box // 2)
    da = own_cols[:, 0:1] - mid
    db = own_cols[:, 1:2] - mid
    radial = da * da + db * db
    kk = lax.broadcasted_iota(jnp.int32, (own, box), 1).astype(F32) - mid
    inside = radial + kk * kk < mid * mid
    loads[1].wait()
    loads[2].wait()
    masked = jnp.concatenate(
        [
            jnp.where(inside, coeffs[0, 0].astype(F32), 0.0).astype(BF),
            jnp.where(inside, coeffs[0, 1].astype(F32), 0.0).astype(BF),
        ],
        axis=1,
    )
    zp = lax.dot_general(z_inv[...], masked, NT, preferred_element_type=F32)
    for z in range(slab):
        send1[z] = zp[2 * z : 2 * z + 2, :].astype(BF)
    gath[me_b] = zp.astype(BF)

    pl.semaphore_wait(barrier, planes - 1 + len(x_peers) + zhi + core)

    def exchange(pick, dst, out, into):
        for peer in far:
            send(pick(peer), dst.at[me_p], out, into, {"pw": peer})

    exchange(lambda peer: send1.at[peer], recv1, 1, 8 + my_z // 2)
    for load in loads[3:]:
        load.start()
    recv1[me_p] = send1[me_p]

    @pl.when(zhi == 1)
    def _():
        forward(me_b, partner, 1)

    for peer in x_peers:
        forward(me_b, peer, 2)

    @pl.when(core == 1)
    def _():
        forward(me_b, sibling, 0)

    level = lax.broadcasted_iota(jnp.int32, (box, own), 0).astype(F32).astype(BF)

    def mark(p):
        at = sticks[p].astype(F32).astype(BF)
        cols = slice(p * own, (p + 1) * own)
        one = jnp.ones((box, own), BF)
        zero = jnp.zeros((box, own), BF)
        hot_a[:, cols] = jnp.where(level == at[0:1, :], one, zero)
        hot_b[:, cols] = jnp.where(level == at[1:2, :], one, zero)

    for p in range(planes):
        mark(p)
    for load in loads[3:]:
        load.wait()

    mine = my_z // 2
    runs = nz // 2
    boxed = jnp.zeros((2 * box, box), F32)
    for k in range(runs):
        if k == 0:
            run = mine
        else:
            up = k - 1 + (k - 1 + runs - mine) // runs
            down = runs - k - (mine + k) // runs
            run = low * up + (1 - low) * down
        arrived(recv1.at[pl.ds(0, 2 * ny - (k == 0))], 8 + run)
        re_cols = []
        im_cols = []
        rhs = []
        for y in range(ny):
            p = y * nz + 2 * run
            cols = pl.ds(pl.multiple_of(p * own, 2 * own), 2 * own)
            hot = hot_a[:, cols]
            at = jnp.concatenate([recv1[p], recv1[p + 1]], axis=1)
            re_cols.append(hot * at[0:1, :])
            im_cols.append(hot * at[1:2, :])
            rhs.append(hot_b[:, cols])
        spread = jnp.concatenate(
            [jnp.concatenate(re_cols, axis=1), jnp.concatenate(im_cols, axis=1)], axis=0
        )
        boxed += lax.dot_general(
            spread, jnp.concatenate(rhs, axis=1), NT, preferred_element_type=F32
        )
    boxed = boxed.astype(BF)
    boxed = jnp.concatenate([boxed[0:box], boxed[box : 2 * box]], axis=1)

    rows = jnp.dot(boxed, y_inv[...], preferred_element_type=F32).astype(BF)
    half[0:box, :] = rows[:, 0:grid]
    half[box : 2 * box, :] = rows[:, grid : 2 * grid]

    for t in range(2 * grid // box):
        tile = slice(t * box, (t + 1) * box)
        lane = slice((t * box) % grid, (t * box) % grid + box)
        field = jnp.dot(x_inv[tile, :], half[...], preferred_element_type=F32)
        prod[tile, :] = (pot[0, lane, :].astype(F32) * field).astype(BF)

    hf = jnp.dot(fwd[...], prod[...], preferred_element_type=F32).astype(BF)
    hf = jnp.concatenate([hf[0:box], hf[box : 2 * box]], axis=1)
    cell = lax.dot_general(fwd[...], hf, NT, preferred_element_type=F32).astype(BF)

    width = 2 * own
    runs = nz // 2
    for k in range(runs):
        run = low * (runs - 1 - k) + (1 - low) * k
        for dy in y_far:
            p = place_of(dy, 2 * run)
            cols = pl.ds(pl.multiple_of(p * own, width), width)
            picked = jnp.dot(cell, hot_a[:, cols], preferred_element_type=F32)
            hot = hot_b[:, cols].astype(F32)
            re = jnp.sum(picked[0:box] * hot, axis=0, keepdims=True)
            im = jnp.sum(picked[box : 2 * box] * hot, axis=0, keepdims=True)
            both = jnp.concatenate([re, im], axis=0).astype(BF)
            for q in range(2):
                send2[p + q] = both[:, q * own : (q + 1) * own]
        for dy in y_far:
            for q in range(2):
                peer = place_of(dy, 2 * run + q)

                def push(peer=peer):
                    send(send2.at[peer], recv2.at[me_p], 2, 6, {"pw": peer})

                if dy:
                    push()
                else:
                    pl.when(peer != me_p)(push)
    recv2[me_p] = send2[me_p]

    arrived(gath.at[0], 0)

    @pl.when(core == 0)
    def _():
        forward(me_b, sibling, 0)

    arrived(gath.at[pl.ds(0, len(x_peers))], 2)
    for peer in x_peers:
        forward(peer, sibling, 4)
    arrived(gath.at[0], 1)

    @pl.when(zhi == 0)
    def _():
        forward(me_b, partner, 1)

    for peer in x_peers:
        forward(partner, peer, 3)
    forward(partner, sibling, 4)
    arrived(gath.at[pl.ds(0, len(x_peers))], 3)
    for peer in x_peers:
        forward(peer + 2 - 4 * zhi, sibling, 4)

    arrived(recv2.at[pl.ds(0, planes - 1)], 6)
    back = jnp.concatenate([recv2[z].astype(F32) for z in range(slab)], axis=0)

    even = lax.rem(lax.broadcasted_iota(jnp.int32, (2 * slab, own), 0), 2) == 0
    turned = jnp.where(
        even, pltpu.roll(back, 2 * slab - 1, axis=0), -pltpu.roll(back, 1, axis=0)
    )
    arrived(gath.at[pl.ds(0, bands // 2 - 1)], 4)
    scale = math.sqrt(box / slab) / math.sqrt(planes * own * box)
    re_rows = []
    im_rows = []
    for i in range(bands):
        other = gath[i].astype(F32)
        re_rows.append(jnp.sum(other * back, axis=0, keepdims=True))
        im_rows.append(jnp.sum(other * turned, axis=0, keepdims=True))
    lanes = jnp.concatenate(re_rows + im_rows, axis=0)
    total = jnp.sum(lanes, axis=1, keepdims=True) * scale
    wide = jnp.concatenate(
        [jnp.broadcast_to(total, (2 * bands, own)), jnp.zeros((own - 2 * bands, own), F32)], axis=0
    )
    part[...] = jnp.transpose(wide)[0:1, :]
    exchange(lambda peer: part, parts, 3, 7)
    parts[me_p] = part[...]

    out = lax.dot_general(back.astype(BF), z_fwd[...], TN, preferred_element_type=F32)
    applied_ref[0, 0] = jnp.where(inside, out[:, 0:box], 0.0).astype(BF)
    applied_ref[0, 1] = jnp.where(inside, out[:, box : 2 * box], 0.0).astype(BF)

    arrived(parts.at[pl.ds(0, planes - 1)], 7)
    summed = jnp.sum(parts[...], axis=0)
    corr_ref[0] = summed[:, 0:bands]
    corr_ref[1] = summed[:, bands : 2 * bands]

    for sem, ref in (
        (0, gath.at[pl.ds(0, bands - 1)]),
        (1, recv1.at[pl.ds(0, planes - 1)]),
        (2, recv2.at[pl.ds(0, planes - 1)]),
        (3, parts.at[pl.ds(0, planes - 1)]),
    ):
        pltpu.make_async_copy(ref, ref, send_sem.at[sem]).wait()


def local(band_coeffs, potential, stick_list):
    bands = lax.axis_size("band")
    planes = lax.axis_size("pw")
    own = band_coeffs.shape[2]
    box = band_coeffs.shape[3]
    grid = potential.shape[1]
    slab = potential.shape[0] * planes
    z_inv, z_fwd, y_inv, x_inv, fwd = (jnp.asarray(t) for t in make_tables(box, grid, slab))
    sticks = stick_list.T.reshape(2, planes, own).transpose(1, 0, 2)
    any_space = pl.BlockSpec(memory_space=pl.ANY)
    vmem = pl.BlockSpec(memory_space=pltpu.VMEM)
    applied, corr = pl.pallas_call(
        functools.partial(kernel, (bands, planes, box, grid, own, slab)),
        out_shape=(
            pltpu.VMEM(band_coeffs.shape, BF),
            pltpu.VMEM((2, 1, bands), F32),
        ),
        in_specs=[any_space] * 8,
        out_specs=(vmem, vmem),
        scratch_shapes=[
            pltpu.VMEM(band_coeffs.shape, BF),
            pltpu.VMEM(potential.shape, BF),
            pltpu.VMEM(sticks.shape, jnp.int32),
            pltpu.VMEM(z_inv.shape, BF),
            pltpu.VMEM(z_fwd.shape, BF),
            pltpu.VMEM(y_inv.shape, BF),
            pltpu.VMEM(x_inv.shape, BF),
            pltpu.VMEM(fwd.shape, BF),
            pltpu.VMEM((box, planes * own), BF),
            pltpu.VMEM((box, planes * own), BF),
            pltpu.VMEM((2 * box, grid), BF),
            pltpu.VMEM((2 * grid, grid), BF),
            pltpu.VMEM((slab, 2, own), BF),
            pltpu.VMEM((planes, 2, own), BF),
            pltpu.VMEM((planes, 2, own), BF),
            pltpu.VMEM((slab, 2, own), BF),
            pltpu.VMEM((bands, 2 * slab, own), BF),
            pltpu.VMEM((1, own), F32),
            pltpu.VMEM((planes, 1, own), F32),
            pltpu.SemaphoreType.DMA((8,)),
            pltpu.SemaphoreType.DMA((4,)),
            pltpu.SemaphoreType.DMA((12,)),
        ],
        compiler_params=pltpu.CompilerParams(
            collective_id=0, has_side_effects=True, vmem_limit_bytes=56 * 1024 * 1024
        ),
        name="local_potential",
    )(band_coeffs, potential, sticks, z_inv, z_fwd, y_inv, x_inv, fwd)
    return applied, corr.transpose(0, 2, 1)


def solution(mesh):
    return jax.shard_map(
        local,
        mesh=mesh,
        in_specs=(P("band", None, "pw", None), P("pw", None, None), P()),
        out_specs=(P("band", None, "pw", None), P(None, None, "band")),
        check_vma=False,
    )
```

```python
import functools
import math

import jax
import jax.numpy as jnp
import ml_dtypes
import numpy as np
from jax import lax
from jax.experimental import pallas as pl
from jax.experimental.pallas import tpu as pltpu
from jax.sharding import PartitionSpec as P

MESH = pl.DeviceIdType.MESH
BF = jnp.bfloat16
F32 = jnp.float32
NT = (((1,), (1,)), ((), ()))
TN = (((0,), (0,)), ((), ()))
RUN = 8


def phase_table(box_count, grid_count, period, sign_value, factor):
    box_index = np.arange(box_count, dtype=np.int64) - box_count // 2
    grid_index = np.arange(grid_count, dtype=np.int64)
    turns = box_index[:, None] * grid_index[None, :] % period
    angles = turns.astype(np.float64) * (2.0 * math.pi / period)
    cos_part = (np.cos(angles) * factor).astype(np.float32).astype(ml_dtypes.bfloat16)
    sin_part = (sign_value * np.sin(angles) * factor).astype(np.float32).astype(ml_dtypes.bfloat16)
    return cos_part, sin_part


def plane_order(slab):
    return [
        y * RUN + 2 * run + q for run in range(RUN // 2) for y in range(slab // RUN) for q in range(2)
    ]


def make_tables(box, grid, slab):
    inv_c, inv_s = phase_table(box, grid, grid, 1.0, 1.0 / math.sqrt(box))
    fwd_c, fwd_s = phase_table(box, grid, grid, -1.0, 1.0 / math.sqrt(grid))
    zi_c, zi_s = phase_table(box, slab, grid, 1.0, 1.0 / math.sqrt(box))
    zf_c, zf_s = phase_table(box, slab, grid, -1.0, 1.0 / math.sqrt(slab))
    order = plane_order(slab)
    zi_c, zi_s, zf_c, zf_s = (t[:, order] for t in (zi_c, zi_s, zf_c, zf_s))
    z_inv = np.stack(
        [np.concatenate([zi_c.T, -zi_s.T], 1), np.concatenate([zi_s.T, zi_c.T], 1)], 1
    ).reshape(2 * slab, 2 * box)
    z_fwd = np.stack(
        [np.concatenate([zf_c.T, zf_s.T], 1), np.concatenate([-zf_s.T, zf_c.T], 1)], 1
    ).reshape(2 * slab, 2 * box)
    y_inv = np.block([[inv_c, inv_s], [-inv_s, inv_c]])
    x_inv = np.block([[inv_c.T, -inv_s.T], [inv_s.T, inv_c.T]])
    x_fwd = np.block([[fwd_c, -fwd_s], [fwd_s, fwd_c]])
    y_fwd = np.block([[fwd_c, -fwd_s], [fwd_s, fwd_c]])
    assert (x_fwd == y_fwd).all()
    return z_inv, z_fwd, y_inv, x_inv, x_fwd


def kernel(
    sizes,
    coeffs_hbm, pot_hbm, sticks_hbm, z_inv_hbm, z_fwd_hbm, y_inv_hbm, x_inv_hbm, fwd_hbm,
    applied_ref, corr_ref,
    coeffs, pot, sticks, z_inv, z_fwd, y_inv, x_inv, fwd,
    hot_a, hot_b, half, prod,
    send1, recv1, send2, recv2, back, gath, part, parts,
    load_sem, send_sem, recv_sem,
):
    bands, planes, box, grid, own, slab = sizes
    me_b = lax.axis_index("band")
    me_p = lax.axis_index("pw")
    nz = RUN
    ny = planes // nz
    my_z = lax.rem(me_p, nz)
    my_y = me_p // nz
    low = 1 - my_z // (nz // 2)
    y_far = sorted(range(ny), key=lambda d: -min(d, ny - d))

    def place_of(dy, z):
        return lax.rem(my_y + dy, ny) * nz + z

    far = []
    for k in range(nz - 1):
        down = nz - 1 - k - (k + my_z) // (nz - 1)
        up = k + (k + nz - my_z) // nz
        far += [place_of(dy, low * down + (1 - low) * up) for dy in y_far]
    far += [place_of(dy, my_z) for dy in y_far if dy]
    core = lax.rem(me_b, 2)
    zhi = lax.rem(me_b // 2, 2)
    xs = bands // 4
    sibling = me_b + 1 - 2 * core
    partner = me_b + 2 - 4 * zhi
    x_peers = [lax.rem(me_b + 4 * d, bands) for d in range(1, xs)]

    barrier = pltpu.get_barrier_semaphore()

    def greet(step, carry):
        pl.semaphore_signal(
            barrier, inc=1, device_id={"pw": lax.rem(me_p + step, planes)}, device_id_type=MESH
        )
        return carry

    lax.fori_loop(1, planes, greet, 0)

    def hello(peer):
        pl.semaphore_signal(barrier, inc=1, device_id={"band": peer}, device_id_type=MESH)

    for peer in x_peers:
        hello(peer)

    @pl.when(zhi == 0)
    def _():
        hello(partner)

    @pl.when(core == 0)
    def _():
        hello(sibling)

    loads = [
        pltpu.make_async_copy(src, dst, load_sem.at[n])
        for n, (src, dst) in enumerate(
            [
                (sticks_hbm, sticks), (coeffs_hbm, coeffs), (z_inv_hbm, z_inv),
                (y_inv_hbm, y_inv), (x_inv_hbm, x_inv), (pot_hbm, pot), (fwd_hbm, fwd), (z_fwd_hbm, z_fwd),
            ]
        )
    ]
    for load in loads[:3]:
        load.start()

    def send(src, dst, out, into, where):
        pltpu.make_async_remote_copy(
            src_ref=src,
            dst_ref=dst,
            send_sem=send_sem.at[out],
            recv_sem=recv_sem.at[into],
            device_id=where,
            device_id_type=MESH,
        ).start()

    def arrived(ref, index):
        pltpu.make_async_copy(ref, ref, recv_sem.at[index]).wait()

    def forward(block, band, into):
        send(gath.at[block], gath.at[block], 0, into, {"band": band})

    loads[0].wait()
    own_cols = jnp.transpose(
        jnp.concatenate([sticks[me_p], jnp.zeros((6, own), jnp.int32)], axis=0).astype(F32)
    )
    mid = float(box // 2)
    da = own_cols[:, 0:1] - mid
    db = own_cols[:, 1:2] - mid
    radial = da * da + db * db
    kk = lax.broadcasted_iota(jnp.int32, (own, box), 1).astype(F32) - mid
    inside = radial + kk * kk < mid * mid
    loads[1].wait()
    loads[2].wait()
    masked = jnp.concatenate(
        [
            jnp.where(inside, coeffs[0, 0].astype(F32), 0.0).astype(BF),
            jnp.where(inside, coeffs[0, 1].astype(F32), 0.0).astype(BF),
        ],
        axis=1,
    )
    zp = lax.dot_general(z_inv[...], masked, NT, preferred_element_type=F32)
    for n, z in enumerate(plane_order(slab)):
        send1[z] = zp[2 * n : 2 * n + 2, :].astype(BF)
    gath[me_b] = zp.astype(BF)

    pl.semaphore_wait(barrier, planes - 1 + len(x_peers) + zhi + core)

    def exchange(pick, dst, out, into):
        for peer in far:
            send(pick(peer), dst.at[me_p], out, into, {"pw": peer})

    exchange(lambda peer: send1.at[peer], recv1, 1, 8 + my_z // 2)
    for load in loads[3:]:
        load.start()
    recv1[me_p] = send1[me_p]

    @pl.when(zhi == 1)
    def _():
        forward(me_b, partner, 1)

    for peer in x_peers:
        forward(me_b, peer, 2)

    @pl.when(core == 1)
    def _():
        forward(me_b, sibling, 0)

    level = lax.broadcasted_iota(jnp.int32, (box, own), 0).astype(F32).astype(BF)

    def mark(p):
        at = sticks[p].astype(F32).astype(BF)
        cols = slice(p * own, (p + 1) * own)
        one = jnp.ones((box, own), BF)
        zero = jnp.zeros((box, own), BF)
        hot_a[:, cols] = jnp.where(level == at[0:1, :], one, zero)
        hot_b[:, cols] = jnp.where(level == at[1:2, :], one, zero)

    for p in range(planes):
        mark(p)
    for load in loads[3:]:
        load.wait()

    mine = my_z // 2
    runs = nz // 2
    nearest = [mine]
    for k in range(1, runs):
        up = k - 1 + (k - 1 + runs - mine) // runs
        down = runs - k - (mine + k) // runs
        nearest.append(low * up + (1 - low) * down)
    boxed = jnp.zeros((2 * box, box), F32)
    for k, run in enumerate(nearest):
        arrived(recv1.at[pl.ds(0, 2 * ny - (k == 0))], 8 + run)
        re_cols = []
        im_cols = []
        rhs = []
        for y in range(ny):
            p = y * nz + 2 * run
            cols = pl.ds(pl.multiple_of(p * own, 2 * own), 2 * own)
            hot = hot_a[:, cols]
            at = jnp.concatenate([recv1[p], recv1[p + 1]], axis=1)
            re_cols.append(hot * at[0:1, :])
            im_cols.append(hot * at[1:2, :])
            rhs.append(hot_b[:, cols])
        spread = jnp.concatenate(
            [jnp.concatenate(re_cols, axis=1), jnp.concatenate(im_cols, axis=1)], axis=0
        )
        boxed += lax.dot_general(
            spread, jnp.concatenate(rhs, axis=1), NT, preferred_element_type=F32
        )
    boxed = boxed.astype(BF)
    boxed = jnp.concatenate([boxed[0:box], boxed[box : 2 * box]], axis=1)

    rows = jnp.dot(boxed, y_inv[...], preferred_element_type=F32).astype(BF)
    half[0:box, :] = rows[:, 0:grid]
    half[box : 2 * box, :] = rows[:, grid : 2 * grid]

    for t in range(2 * grid // box):
        tile = slice(t * box, (t + 1) * box)
        lane = slice((t * box) % grid, (t * box) % grid + box)
        field = jnp.dot(x_inv[tile, :], half[...], preferred_element_type=F32)
        prod[tile, :] = (pot[0, lane, :].astype(F32) * field).astype(BF)

    hf = jnp.dot(fwd[...], prod[...], preferred_element_type=F32).astype(BF)
    hf = jnp.concatenate([hf[0:box], hf[box : 2 * box]], axis=1)
    def pass_on():
        arrived(gath.at[0], 1)

        @pl.when(zhi == 0)
        def _():
            forward(me_b, partner, 1)

        for peer in x_peers:
            forward(partner, peer, 3)

    @pl.when(zhi == 0)
    def _():
        pass_on()

    cell = lax.dot_general(fwd[...], hf, NT, preferred_element_type=F32).astype(BF)

    width = 2 * own
    for k in range(runs):
        run = low * (runs - 1 - k) + (1 - low) * k
        for dy in y_far:
            p = place_of(dy, 2 * run)
            cols = pl.ds(pl.multiple_of(p * own, width), width)
            picked = jnp.dot(cell, hot_a[:, cols], preferred_element_type=F32)
            hot = hot_b[:, cols].astype(F32)
            re = jnp.sum(picked[0:box] * hot, axis=0, keepdims=True)
            im = jnp.sum(picked[box : 2 * box] * hot, axis=0, keepdims=True)
            both = jnp.concatenate([re, im], axis=0).astype(BF)
            for q in range(2):
                send2[p + q] = both[:, q * own : (q + 1) * own]
        for dy in y_far:
            for q in range(2):
                peer = place_of(dy, 2 * run + q)

                def push(peer=peer):
                    send(send2.at[peer], recv2.at[me_p], 2, 12 + mine, {"pw": peer})

                if dy:
                    push()
                else:
                    pl.when(peer != me_p)(push)
    recv2[me_p] = send2[me_p]

    arrived(gath.at[0], 0)

    @pl.when(core == 0)
    def _():
        forward(me_b, sibling, 0)

    arrived(gath.at[pl.ds(0, len(x_peers))], 2)
    for peer in x_peers:
        forward(peer, sibling, 4)
    @pl.when(zhi == 1)
    def _():
        pass_on()

    forward(partner, sibling, 4)
    arrived(gath.at[pl.ds(0, len(x_peers))], 3)
    for peer in x_peers:
        forward(peer + 2 - 4 * zhi, sibling, 4)

    arrived(gath.at[pl.ds(0, bands // 2 - 1)], 4)

    span = 4 * ny
    even = lax.rem(lax.broadcasted_iota(jnp.int32, (span, own), 0), 2) == 0
    re_sum = [jnp.zeros((8, own), F32)] * bands
    im_sum = [jnp.zeros((8, own), F32)] * bands
    for k, run in enumerate(nearest):
        arrived(recv2.at[pl.ds(0, 2 * ny - (k == 0))], 12 + run)
        got = [recv2[y * nz + 2 * run + q].astype(F32) for y in range(ny) for q in range(2)]
        here = jnp.concatenate(got, axis=0)
        turned = jnp.where(
            even, pltpu.roll(here, span - 1, axis=0), -pltpu.roll(here, 1, axis=0)
        )
        rows = pl.ds(pl.multiple_of(run * span, span), span)
        back[rows, :] = here.astype(BF)
        for i in range(bands):
            other = gath[i, rows, :].astype(F32)
            by_re = other * here
            by_im = other * turned
            for t in range(0, span, 8):
                re_sum[i] = re_sum[i] + by_re[t : t + 8]
                im_sum[i] = im_sum[i] + by_im[t : t + 8]
    scale = math.sqrt(box / slab) / math.sqrt(planes * own * box)
    lanes = jnp.concatenate(
        [jnp.sum(t, axis=0, keepdims=True) for t in re_sum + im_sum], axis=0
    )
    total = jnp.sum(lanes, axis=1, keepdims=True) * scale
    on_lane = lax.broadcasted_iota(jnp.int32, (2 * bands, own), 0) == lax.broadcasted_iota(
        jnp.int32, (2 * bands, own), 1
    )
    part[...] = jnp.sum(jnp.where(on_lane, total, 0.0), axis=0, keepdims=True)
    exchange(lambda peer: part, parts, 3, 7)
    parts[me_p] = part[...]

    out = lax.dot_general(back[...], z_fwd[...], TN, preferred_element_type=F32)
    applied_ref[0, 0] = jnp.where(inside, out[:, 0:box], 0.0).astype(BF)
    applied_ref[0, 1] = jnp.where(inside, out[:, box : 2 * box], 0.0).astype(BF)

    arrived(parts.at[pl.ds(0, planes - 1)], 7)
    summed = jnp.sum(parts[...], axis=0)
    corr_ref[0] = summed[:, 0:bands]
    corr_ref[1] = summed[:, bands : 2 * bands]

    for sem, ref in (
        (0, gath.at[pl.ds(0, bands - 1)]),
        (1, recv1.at[pl.ds(0, planes - 1)]),
        (2, recv2.at[pl.ds(0, planes - 1)]),
        (3, parts.at[pl.ds(0, planes - 1)]),
    ):
        pltpu.make_async_copy(ref, ref, send_sem.at[sem]).wait()


def local(band_coeffs, potential, stick_list):
    bands = lax.axis_size("band")
    planes = lax.axis_size("pw")
    own = band_coeffs.shape[2]
    box = band_coeffs.shape[3]
    grid = potential.shape[1]
    slab = potential.shape[0] * planes
    z_inv, z_fwd, y_inv, x_inv, fwd = (jnp.asarray(t) for t in make_tables(box, grid, slab))
    sticks = stick_list.T.reshape(2, planes, own).transpose(1, 0, 2)
    any_space = pl.BlockSpec(memory_space=pl.ANY)
    vmem = pl.BlockSpec(memory_space=pltpu.VMEM)
    applied, corr = pl.pallas_call(
        functools.partial(kernel, (bands, planes, box, grid, own, slab)),
        out_shape=(
            pltpu.VMEM(band_coeffs.shape, BF),
            pltpu.VMEM((2, 1, bands), F32),
        ),
        in_specs=[any_space] * 8,
        out_specs=(vmem, vmem),
        scratch_shapes=[
            pltpu.VMEM(band_coeffs.shape, BF),
            pltpu.VMEM(potential.shape, BF),
            pltpu.VMEM(sticks.shape, jnp.int32),
            pltpu.VMEM(z_inv.shape, BF),
            pltpu.VMEM(z_fwd.shape, BF),
            pltpu.VMEM(y_inv.shape, BF),
            pltpu.VMEM(x_inv.shape, BF),
            pltpu.VMEM(fwd.shape, BF),
            pltpu.VMEM((box, planes * own), BF),
            pltpu.VMEM((box, planes * own), BF),
            pltpu.VMEM((2 * box, grid), BF),
            pltpu.VMEM((2 * grid, grid), BF),
            pltpu.VMEM((slab, 2, own), BF),
            pltpu.VMEM((planes, 2, own), BF),
            pltpu.VMEM((planes, 2, own), BF),
            pltpu.VMEM((slab, 2, own), BF),
            pltpu.VMEM((2 * slab, own), BF),
            pltpu.VMEM((bands, 2 * slab, own), BF),
            pltpu.VMEM((1, own), F32),
            pltpu.VMEM((planes, 1, own), F32),
            pltpu.SemaphoreType.DMA((8,)),
            pltpu.SemaphoreType.DMA((4,)),
            pltpu.SemaphoreType.DMA((16,)),
        ],
        compiler_params=pltpu.CompilerParams(
            collective_id=0, has_side_effects=True, vmem_limit_bytes=56 * 1024 * 1024
        ),
        name="local_potential",
    )(band_coeffs, potential, sticks, z_inv, z_fwd, y_inv, x_inv, fwd)
    return applied, corr.transpose(0, 2, 1)


def solution(mesh):
    return jax.shard_map(
        local,
        mesh=mesh,
        in_specs=(P("band", None, "pw", None), P("pw", None, None), P()),
        out_specs=(P("band", None, "pw", None), P(None, None, "band")),
        check_vma=False,
    )
```

```python
import functools
import math

import jax
import jax.numpy as jnp
import ml_dtypes
import numpy as np
from jax import lax
from jax.experimental import pallas as pl
from jax.experimental.pallas import tpu as pltpu
from jax.sharding import PartitionSpec as P

MESH = pl.DeviceIdType.MESH
BF = jnp.bfloat16
F32 = jnp.float32
NT = (((1,), (1,)), ((), ()))
TN = (((0,), (0,)), ((), ()))
RUN = 8


def phase_table(box_count, grid_count, period, sign_value, factor):
    box_index = np.arange(box_count, dtype=np.int64) - box_count // 2
    grid_index = np.arange(grid_count, dtype=np.int64)
    turns = box_index[:, None] * grid_index[None, :] % period
    angles = turns.astype(np.float64) * (2.0 * math.pi / period)
    cos_part = (np.cos(angles) * factor).astype(np.float32).astype(ml_dtypes.bfloat16)
    sin_part = (sign_value * np.sin(angles) * factor).astype(np.float32).astype(ml_dtypes.bfloat16)
    return cos_part, sin_part


def plane_order(slab):
    return [
        y * RUN + 2 * run + q for run in range(RUN // 2) for y in range(slab // RUN) for q in range(2)
    ]


def make_tables(box, grid, slab):
    inv_c, inv_s = phase_table(box, grid, grid, 1.0, 1.0 / math.sqrt(box))
    fwd_c, fwd_s = phase_table(box, grid, grid, -1.0, 1.0 / math.sqrt(grid))
    zi_c, zi_s = phase_table(box, slab, grid, 1.0, 1.0 / math.sqrt(box))
    zf_c, zf_s = phase_table(box, slab, grid, -1.0, 1.0 / math.sqrt(slab))
    order = plane_order(slab)
    zi_c, zi_s, zf_c, zf_s = (t[:, order] for t in (zi_c, zi_s, zf_c, zf_s))
    z_inv = np.stack(
        [np.concatenate([zi_c.T, -zi_s.T], 1), np.concatenate([zi_s.T, zi_c.T], 1)], 1
    ).reshape(2 * slab, 2 * box)
    z_fwd = np.stack(
        [np.concatenate([zf_c.T, zf_s.T], 1), np.concatenate([-zf_s.T, zf_c.T], 1)], 1
    ).reshape(2 * slab, 2 * box)
    split = [(slice(first, None, 2), slice(0, grid // 2)) for first in range(2)]
    inv = [(inv_c[at], inv_s[at]) for at in split]
    fwd = [(fwd_c[at], fwd_s[at]) for at in split]
    y_inv = np.concatenate([np.block([[c, s], [-s, c]]) for c, s in inv])
    x_inv = np.concatenate([np.block([[c.T, -s.T], [s.T, c.T]]) for c, s in inv])
    fwd = np.concatenate([np.block([[c, -s], [s, c]]) for c, s in fwd])
    return z_inv, z_fwd, y_inv, x_inv, fwd


def kernel(
    sizes,
    coeffs_hbm, pot_hbm, sticks_hbm, z_inv_hbm, z_fwd_hbm, y_inv_hbm, x_inv_hbm, fwd_hbm,
    applied_ref, corr_ref,
    coeffs, pot, sticks, z_inv, z_fwd, y_inv, x_inv, fwd,
    hot_a, hot_b, half, prod,
    send1, recv1, send2, recv2, back, gath, part, parts,
    load_sem, send_sem, recv_sem,
):
    bands, planes, box, grid, own, slab = sizes
    me_b = lax.axis_index("band")
    me_p = lax.axis_index("pw")
    nz = RUN
    ny = planes // nz
    my_z = lax.rem(me_p, nz)
    my_y = me_p // nz
    low = 1 - my_z // (nz // 2)
    y_far = sorted(range(ny), key=lambda d: -min(d, ny - d))

    def place_of(dy, z):
        return lax.rem(my_y + dy, ny) * nz + z

    far = []
    for k in range(nz - 1):
        down = nz - 1 - k - (k + my_z) // (nz - 1)
        up = k + (k + nz - my_z) // nz
        far += [place_of(dy, low * down + (1 - low) * up) for dy in y_far]
    far += [place_of(dy, my_z) for dy in y_far if dy]
    core = lax.rem(me_b, 2)
    zhi = lax.rem(me_b // 2, 2)
    xs = bands // 4
    sibling = me_b + 1 - 2 * core
    partner = me_b + 2 - 4 * zhi
    x_peers = [lax.rem(me_b + 4 * d, bands) for d in range(1, xs)]

    barrier = pltpu.get_barrier_semaphore()

    def greet(step, carry):
        pl.semaphore_signal(
            barrier, inc=1, device_id={"pw": lax.rem(me_p + step, planes)}, device_id_type=MESH
        )
        return carry

    lax.fori_loop(1, planes, greet, 0)

    def hello(peer):
        pl.semaphore_signal(barrier, inc=1, device_id={"band": peer}, device_id_type=MESH)

    for peer in x_peers:
        hello(peer)

    @pl.when(zhi == 0)
    def _():
        hello(partner)

    @pl.when(core == 0)
    def _():
        hello(sibling)

    loads = [
        pltpu.make_async_copy(src, dst, load_sem.at[n])
        for n, (src, dst) in enumerate(
            [
                (sticks_hbm, sticks), (coeffs_hbm, coeffs), (z_inv_hbm, z_inv),
                (y_inv_hbm, y_inv), (x_inv_hbm, x_inv), (pot_hbm, pot), (fwd_hbm, fwd), (z_fwd_hbm, z_fwd),
            ]
        )
    ]
    for load in loads[:3]:
        load.start()

    def send(src, dst, out, into, where):
        pltpu.make_async_remote_copy(
            src_ref=src,
            dst_ref=dst,
            send_sem=send_sem.at[out],
            recv_sem=recv_sem.at[into],
            device_id=where,
            device_id_type=MESH,
        ).start()

    def arrived(ref, index):
        pltpu.make_async_copy(ref, ref, recv_sem.at[index]).wait()

    def forward(block, band, into):
        send(gath.at[block], gath.at[block], 0, into, {"band": band})

    loads[0].wait()
    own_cols = jnp.transpose(
        jnp.concatenate([sticks[me_p], jnp.zeros((6, own), jnp.int32)], axis=0).astype(F32)
    )
    mid = float(box // 2)
    da = own_cols[:, 0:1] - mid
    db = own_cols[:, 1:2] - mid
    radial = da * da + db * db
    kk = lax.broadcasted_iota(jnp.int32, (own, box), 1).astype(F32) - mid
    inside = radial + kk * kk < mid * mid
    loads[1].wait()
    loads[2].wait()
    masked = jnp.concatenate(
        [
            jnp.where(inside, coeffs[0, 0].astype(F32), 0.0).astype(BF),
            jnp.where(inside, coeffs[0, 1].astype(F32), 0.0).astype(BF),
        ],
        axis=1,
    )
    zp = lax.dot_general(z_inv[...], masked, NT, preferred_element_type=F32)
    for n, z in enumerate(plane_order(slab)):
        send1[z] = zp[2 * n : 2 * n + 2, :].astype(BF)
    gath[me_b] = zp.astype(BF)

    pl.semaphore_wait(barrier, planes - 1 + len(x_peers) + zhi + core)

    def exchange(pick, dst, out, into):
        for peer in far:
            send(pick(peer), dst.at[me_p], out, into, {"pw": peer})

    @pl.when(zhi == 1)
    def _():
        forward(me_b, partner, 1)

    exchange(lambda peer: send1.at[peer], recv1, 1, 8 + my_z // 2)
    for load in loads[3:]:
        load.start()
    recv1[me_p] = send1[me_p]

    for peer in x_peers:
        forward(me_b, peer, 2)

    @pl.when(core == 1)
    def _():
        forward(me_b, sibling, 0)

    row = lax.broadcasted_iota(jnp.int32, (box, own), 0)
    level = jnp.where(row < box // 2, 2 * row, 2 * row - (box - 1)).astype(F32).astype(BF)

    def mark(p):
        at = sticks[p].astype(F32).astype(BF)
        cols = slice(p * own, (p + 1) * own)
        one = jnp.ones((box, own), BF)
        zero = jnp.zeros((box, own), BF)
        hot_a[:, cols] = jnp.where(level == at[0:1, :], one, zero)
        hot_b[:, cols] = jnp.where(level == at[1:2, :], one, zero)

    for p in range(planes):
        mark(p)
    for load in loads[3:]:
        load.wait()

    mine = my_z // 2
    runs = nz // 2
    nearest = [mine]
    for k in range(1, runs):
        up = k - 1 + (k - 1 + runs - mine) // runs
        down = runs - k - (mine + k) // runs
        nearest.append(low * up + (1 - low) * down)
    boxed = jnp.zeros((2 * box, box), F32)
    for k, run in enumerate(nearest):
        arrived(recv1.at[pl.ds(0, 2 * ny - (k == 0))], 8 + run)
        re_cols = []
        im_cols = []
        rhs = []
        for y in range(ny):
            p = y * nz + 2 * run
            cols = pl.ds(pl.multiple_of(p * own, 2 * own), 2 * own)
            hot = hot_a[:, cols]
            at = jnp.concatenate([recv1[p], recv1[p + 1]], axis=1)
            re_cols.append(hot * at[0:1, :])
            im_cols.append(hot * at[1:2, :])
            rhs.append(hot_b[:, cols])
        spread = jnp.concatenate(
            [jnp.concatenate(re_cols, axis=1), jnp.concatenate(im_cols, axis=1)], axis=0
        )
        boxed += lax.dot_general(
            spread, jnp.concatenate(rhs, axis=1), NT, preferred_element_type=F32
        )
    boxed = boxed.astype(BF)
    hb = box // 2
    hg = grid // 2

    y_half = [
        jnp.dot(
            jnp.concatenate([boxed[0:box, n * hb : (n + 1) * hb], boxed[box:, n * hb : (n + 1) * hb]], axis=1),
            y_inv[n * box : (n + 1) * box, :],
            preferred_element_type=F32,
        )
        for n in range(2)
    ]
    near = (y_half[0] + y_half[1]).astype(BF)
    over = (y_half[0] - y_half[1]).astype(BF)
    for n in range(2):
        for t in range(2):
            rows = slice(n * box + t * hb, n * box + (t + 1) * hb)
            half[rows, 0:hg] = near[n * hb : (n + 1) * hb, t * hg : (t + 1) * hg]
            half[rows, hg:grid] = over[n * hb : (n + 1) * hb, t * hg : (t + 1) * hg]

    for t in range(2):
        x_half = [
            jnp.dot(
                x_inv[n * grid + t * hg : n * grid + (t + 1) * hg, :],
                half[n * box : (n + 1) * box, :],
                preferred_element_type=F32,
            )
            for n in range(2)
        ]
        one = pot[0, 0:hg, :].astype(F32) * (x_half[0] + x_half[1])
        two = pot[0, hg:grid, :].astype(F32) * (x_half[0] - x_half[1])
        prod[t * hg : (t + 1) * hg, :] = (one + two).astype(BF)
        prod[grid + t * hg : grid + (t + 1) * hg, :] = (one - two).astype(BF)

    plus = []
    minus = []
    for n in range(2):
        hf = jnp.dot(
            fwd[n * box : (n + 1) * box, :],
            prod[n * grid : (n + 1) * grid, :],
            preferred_element_type=F32,
        )
        add = (hf[:, 0:hg] + hf[:, hg:grid]).astype(BF)
        sub = (hf[:, 0:hg] - hf[:, hg:grid]).astype(BF)
        plus.append(jnp.concatenate([add[0:hb], add[hb:box]], axis=1))
        minus.append(jnp.concatenate([sub[0:hb], sub[hb:box]], axis=1))

    def pass_on():
        arrived(gath.at[0], 1)

        @pl.when(zhi == 0)
        def _():
            forward(me_b, partner, 1)

        for peer in x_peers:
            forward(partner, peer, 3)

    @pl.when(zhi == 0)
    def _():
        pass_on()

    cells = [
        lax.dot_general(
            fwd[n * box : (n + 1) * box, :],
            jnp.concatenate(side, axis=0),
            NT,
            preferred_element_type=F32,
        ).astype(BF)
        for n, side in enumerate((plus, minus))
    ]
    cell = jnp.concatenate(
        [cells[0][0:hb], cells[1][0:hb], cells[0][hb:box], cells[1][hb:box]], axis=0
    )

    width = 2 * own
    for k in range(runs):
        run = low * (runs - 1 - k) + (1 - low) * k
        for dy in y_far:
            p = place_of(dy, 2 * run)
            cols = pl.ds(pl.multiple_of(p * own, width), width)
            picked = jnp.dot(cell, hot_a[:, cols], preferred_element_type=F32)
            hot = hot_b[:, cols].astype(F32)
            re = jnp.sum(picked[0:box] * hot, axis=0, keepdims=True)
            im = jnp.sum(picked[box : 2 * box] * hot, axis=0, keepdims=True)
            both = jnp.concatenate([re, im], axis=0).astype(BF)
            for q in range(2):
                send2[p + q] = both[:, q * own : (q + 1) * own]
        for dy in y_far:
            for q in range(2):
                peer = place_of(dy, 2 * run + q)

                def push(peer=peer):
                    send(send2.at[peer], recv2.at[me_p], 2, 12 + mine, {"pw": peer})

                if dy:
                    push()
                else:
                    pl.when(peer != me_p)(push)
    recv2[me_p] = send2[me_p]

    arrived(gath.at[0], 0)

    @pl.when(core == 0)
    def _():
        forward(me_b, sibling, 0)

    arrived(gath.at[pl.ds(0, len(x_peers))], 2)
    for peer in x_peers:
        forward(peer, sibling, 4)
    @pl.when(zhi == 1)
    def _():
        pass_on()

    forward(partner, sibling, 4)
    arrived(gath.at[pl.ds(0, len(x_peers))], 3)
    for peer in x_peers:
        forward(peer + 2 - 4 * zhi, sibling, 4)

    arrived(gath.at[pl.ds(0, bands // 2 - 1)], 4)

    span = 4 * ny
    even = lax.rem(lax.broadcasted_iota(jnp.int32, (span, own), 0), 2) == 0
    re_sum = [jnp.zeros((8, own), F32)] * bands
    im_sum = [jnp.zeros((8, own), F32)] * bands
    for k, run in enumerate(nearest):
        arrived(recv2.at[pl.ds(0, 2 * ny - (k == 0))], 12 + run)
        got = [recv2[y * nz + 2 * run + q].astype(F32) for y in range(ny) for q in range(2)]
        here = jnp.concatenate(got, axis=0)
        turned = jnp.where(
            even, pltpu.roll(here, span - 1, axis=0), -pltpu.roll(here, 1, axis=0)
        )
        rows = pl.ds(pl.multiple_of(run * span, span), span)
        back[rows, :] = here.astype(BF)
        for i in range(bands):
            other = gath[i, rows, :].astype(F32)
            by_re = other * here
            by_im = other * turned
            for t in range(0, span, 8):
                re_sum[i] = re_sum[i] + by_re[t : t + 8]
                im_sum[i] = im_sum[i] + by_im[t : t + 8]
    scale = math.sqrt(box / slab) / math.sqrt(planes * own * box)
    lanes = jnp.concatenate(
        [jnp.sum(t, axis=0, keepdims=True) for t in re_sum + im_sum], axis=0
    )
    total = jnp.sum(lanes, axis=1, keepdims=True) * scale
    on_lane = lax.broadcasted_iota(jnp.int32, (2 * bands, own), 0) == lax.broadcasted_iota(
        jnp.int32, (2 * bands, own), 1
    )
    part[...] = jnp.sum(jnp.where(on_lane, total, 0.0), axis=0, keepdims=True)
    exchange(lambda peer: part, parts, 3, 7)
    parts[me_p] = part[...]

    out = lax.dot_general(back[...], z_fwd[...], TN, preferred_element_type=F32)
    applied_ref[0, 0] = jnp.where(inside, out[:, 0:box], 0.0).astype(BF)
    applied_ref[0, 1] = jnp.where(inside, out[:, box : 2 * box], 0.0).astype(BF)

    arrived(parts.at[pl.ds(0, planes - 1)], 7)
    summed = jnp.sum(parts[...], axis=0)
    corr_ref[0] = summed[:, 0:bands]
    corr_ref[1] = summed[:, bands : 2 * bands]

    for sem, ref in (
        (0, gath.at[pl.ds(0, bands - 1)]),
        (1, recv1.at[pl.ds(0, planes - 1)]),
        (2, recv2.at[pl.ds(0, planes - 1)]),
        (3, parts.at[pl.ds(0, planes - 1)]),
    ):
        pltpu.make_async_copy(ref, ref, send_sem.at[sem]).wait()


def local(band_coeffs, potential, stick_list):
    bands = lax.axis_size("band")
    planes = lax.axis_size("pw")
    own = band_coeffs.shape[2]
    box = band_coeffs.shape[3]
    grid = potential.shape[1]
    slab = potential.shape[0] * planes
    z_inv, z_fwd, y_inv, x_inv, fwd = (jnp.asarray(t) for t in make_tables(box, grid, slab))
    sticks = stick_list.T.reshape(2, planes, own).transpose(1, 0, 2)
    any_space = pl.BlockSpec(memory_space=pl.ANY)
    vmem = pl.BlockSpec(memory_space=pltpu.VMEM)
    applied, corr = pl.pallas_call(
        functools.partial(kernel, (bands, planes, box, grid, own, slab)),
        out_shape=(
            pltpu.VMEM(band_coeffs.shape, BF),
            pltpu.VMEM((2, 1, bands), F32),
        ),
        in_specs=[any_space] * 8,
        out_specs=(vmem, vmem),
        scratch_shapes=[
            pltpu.VMEM(band_coeffs.shape, BF),
            pltpu.VMEM(potential.shape, BF),
            pltpu.VMEM(sticks.shape, jnp.int32),
            pltpu.VMEM(z_inv.shape, BF),
            pltpu.VMEM(z_fwd.shape, BF),
            pltpu.VMEM(y_inv.shape, BF),
            pltpu.VMEM(x_inv.shape, BF),
            pltpu.VMEM(fwd.shape, BF),
            pltpu.VMEM((box, planes * own), BF),
            pltpu.VMEM((box, planes * own), BF),
            pltpu.VMEM((2 * box, grid), BF),
            pltpu.VMEM((2 * grid, grid), BF),
            pltpu.VMEM((slab, 2, own), BF),
            pltpu.VMEM((planes, 2, own), BF),
            pltpu.VMEM((planes, 2, own), BF),
            pltpu.VMEM((slab, 2, own), BF),
            pltpu.VMEM((2 * slab, own), BF),
            pltpu.VMEM((bands, 2 * slab, own), BF),
            pltpu.VMEM((1, own), F32),
            pltpu.VMEM((planes, 1, own), F32),
            pltpu.SemaphoreType.DMA((8,)),
            pltpu.SemaphoreType.DMA((4,)),
            pltpu.SemaphoreType.DMA((16,)),
        ],
        compiler_params=pltpu.CompilerParams(
            collective_id=0, has_side_effects=True, vmem_limit_bytes=56 * 1024 * 1024
        ),
        name="local_potential",
    )(band_coeffs, potential, sticks, z_inv, z_fwd, y_inv, x_inv, fwd)
    return applied, corr.transpose(0, 2, 1)


def solution(mesh):
    return jax.shard_map(
        local,
        mesh=mesh,
        in_specs=(P("band", None, "pw", None), P("pw", None, None), P()),
        out_specs=(P("band", None, "pw", None), P(None, None, "band")),
        check_vma=False,
    )
```

```python
import functools
import math

import jax
import jax.numpy as jnp
import ml_dtypes
import numpy as np
from jax import lax
from jax.experimental import pallas as pl
from jax.experimental.pallas import tpu as pltpu
from jax.sharding import PartitionSpec as P

MESH = pl.DeviceIdType.MESH
BF = jnp.bfloat16
F32 = jnp.float32
NT = (((1,), (1,)), ((), ()))
TN = (((0,), (0,)), ((), ()))
RUN = 8


def phase_table(box_count, grid_count, period, sign_value, factor):
    box_index = np.arange(box_count, dtype=np.int64) - box_count // 2
    grid_index = np.arange(grid_count, dtype=np.int64)
    turns = box_index[:, None] * grid_index[None, :] % period
    angles = turns.astype(np.float64) * (2.0 * math.pi / period)
    cos_part = (np.cos(angles) * factor).astype(np.float32).astype(ml_dtypes.bfloat16)
    sin_part = (sign_value * np.sin(angles) * factor).astype(np.float32).astype(ml_dtypes.bfloat16)
    return cos_part, sin_part


def plane_order(slab):
    return [
        y * RUN + 2 * run + q for run in range(RUN // 2) for y in range(slab // RUN) for q in range(2)
    ]


def make_tables(box, grid, slab):
    inv_c, inv_s = phase_table(box, grid, grid, 1.0, 1.0 / math.sqrt(box))
    fwd_c, fwd_s = phase_table(box, grid, grid, -1.0, 1.0 / math.sqrt(grid))
    zi_c, zi_s = phase_table(box, slab, grid, 1.0, 1.0 / math.sqrt(box))
    zf_c, zf_s = phase_table(box, slab, grid, -1.0, 1.0 / math.sqrt(slab))
    order = plane_order(slab)
    zi_c, zi_s, zf_c, zf_s = (t[:, order] for t in (zi_c, zi_s, zf_c, zf_s))
    z_inv = np.stack(
        [np.concatenate([zi_c.T, -zi_s.T], 1), np.concatenate([zi_s.T, zi_c.T], 1)], 1
    ).reshape(2 * slab, 2 * box)
    z_fwd = np.stack(
        [np.concatenate([zf_c.T, zf_s.T], 1), np.concatenate([-zf_s.T, zf_c.T], 1)], 1
    ).reshape(2 * slab, 2 * box)
    split = [(slice(first, None, 2), slice(0, grid // 2)) for first in range(2)]
    inv = [(inv_c[at], inv_s[at]) for at in split]
    fwd = [(fwd_c[at], fwd_s[at]) for at in split]
    y_inv = np.concatenate([np.block([[c, s], [-s, c]]) for c, s in inv])
    x_inv = np.concatenate([np.block([[c.T, -s.T], [s.T, c.T]]) for c, s in inv])
    fwd = np.concatenate([np.block([[c, -s], [s, c]]) for c, s in fwd])
    return z_inv, z_fwd, y_inv, x_inv, fwd


def kernel(
    sizes,
    coeffs_hbm, pot_hbm, sticks_hbm, z_inv_hbm, z_fwd_hbm, y_inv_hbm, x_inv_hbm, fwd_hbm,
    applied_ref, corr_ref,
    coeffs, pot, sticks, z_inv, z_fwd, y_inv, x_inv, fwd,
    hot_a, hot_b, half, prod,
    send1, recv1, send2, recv2, back, gath, part, parts,
    load_sem, send_sem, recv_sem,
):
    bands, planes, box, grid, own, slab = sizes
    me_b = lax.axis_index("band")
    me_p = lax.axis_index("pw")
    nz = RUN
    ny = planes // nz
    my_z = lax.rem(me_p, nz)
    my_y = me_p // nz
    low = 1 - my_z // (nz // 2)
    y_far = sorted(range(ny), key=lambda d: -min(d, ny - d))

    def place_of(dy, z):
        return lax.rem(my_y + dy, ny) * nz + z

    far = []
    for k in range(nz - 1):
        down = nz - 1 - k - (k + my_z) // (nz - 1)
        up = k + (k + nz - my_z) // nz
        far += [place_of(dy, low * down + (1 - low) * up) for dy in y_far]
    far += [place_of(dy, my_z) for dy in y_far if dy]
    core = lax.rem(me_b, 2)
    zhi = lax.rem(me_b // 2, 2)
    xs = bands // 4
    sibling = me_b + 1 - 2 * core
    partner = me_b + 2 - 4 * zhi
    x_peers = [lax.rem(me_b + 4 * d, bands) for d in range(1, xs)]

    barrier = pltpu.get_barrier_semaphore()

    for peer in far:
        pl.semaphore_signal(barrier, inc=1, device_id={"pw": peer}, device_id_type=MESH)

    def hello(peer):
        pl.semaphore_signal(barrier, inc=1, device_id={"band": peer}, device_id_type=MESH)

    for peer in x_peers:
        hello(peer)

    @pl.when(zhi == 0)
    def _():
        hello(partner)

    @pl.when(core == 0)
    def _():
        hello(sibling)

    loads = [
        pltpu.make_async_copy(src, dst, load_sem.at[n])
        for n, (src, dst) in enumerate(
            [
                (sticks_hbm, sticks), (coeffs_hbm, coeffs), (z_inv_hbm, z_inv),
                (y_inv_hbm, y_inv), (x_inv_hbm, x_inv), (pot_hbm, pot), (fwd_hbm, fwd), (z_fwd_hbm, z_fwd),
            ]
        )
    ]
    for load in loads[:3]:
        load.start()

    def send(src, dst, out, into, where):
        pltpu.make_async_remote_copy(
            src_ref=src,
            dst_ref=dst,
            send_sem=send_sem.at[out],
            recv_sem=recv_sem.at[into],
            device_id=where,
            device_id_type=MESH,
        ).start()

    def arrived(ref, index):
        pltpu.make_async_copy(ref, ref, recv_sem.at[index]).wait()

    def forward(block, band, into):
        send(gath.at[block], gath.at[block], 0, into, {"band": band})

    loads[0].wait()
    own_cols = jnp.transpose(
        jnp.concatenate([sticks[me_p], jnp.zeros((6, own), jnp.int32)], axis=0).astype(F32)
    )
    mid = float(box // 2)
    da = own_cols[:, 0:1] - mid
    db = own_cols[:, 1:2] - mid
    radial = da * da + db * db
    kk = lax.broadcasted_iota(jnp.int32, (own, box), 1).astype(F32) - mid
    inside = radial + kk * kk < mid * mid
    loads[1].wait()
    loads[2].wait()
    masked = jnp.concatenate(
        [
            jnp.where(inside, coeffs[0, 0].astype(F32), 0.0).astype(BF),
            jnp.where(inside, coeffs[0, 1].astype(F32), 0.0).astype(BF),
        ],
        axis=1,
    )
    zp = lax.dot_general(z_inv[...], masked, NT, preferred_element_type=F32)
    for n, z in enumerate(plane_order(slab)):
        send1[z] = zp[2 * n : 2 * n + 2, :].astype(BF)
    gath[me_b] = zp.astype(BF)

    pl.semaphore_wait(barrier, planes - 1 + len(x_peers) + zhi + core)

    def exchange(pick, dst, out, into):
        for peer in far:
            send(pick(peer), dst.at[me_p], out, into, {"pw": peer})

    @pl.when(zhi == 1)
    def _():
        forward(me_b, partner, 1)

    exchange(lambda peer: send1.at[peer], recv1, 1, 8 + my_z // 2)
    for load in loads[3:]:
        load.start()
    recv1[me_p] = send1[me_p]

    for peer in x_peers:
        forward(me_b, peer, 2)

    @pl.when(core == 1)
    def _():
        forward(me_b, sibling, 0)

    row = lax.broadcasted_iota(jnp.int32, (box, own), 0)
    level = jnp.where(row < box // 2, 2 * row, 2 * row - (box - 1)).astype(F32).astype(BF)

    def mark(p):
        at = sticks[p].astype(F32).astype(BF)
        cols = slice(p * own, (p + 1) * own)
        one = jnp.ones((box, own), BF)
        zero = jnp.zeros((box, own), BF)
        hot_a[:, cols] = jnp.where(level == at[0:1, :], one, zero)
        hot_b[:, cols] = jnp.where(level == at[1:2, :], one, zero)

    for p in range(planes):
        mark(p)
    for load in loads[3:]:
        load.wait()

    mine = my_z // 2
    runs = nz // 2
    nearest = [mine]
    for k in range(1, runs):
        up = k - 1 + (k - 1 + runs - mine) // runs
        down = runs - k - (mine + k) // runs
        nearest.append(low * up + (1 - low) * down)
    boxed = jnp.zeros((2 * box, box), F32)
    for k, run in enumerate(nearest):
        arrived(recv1.at[pl.ds(0, 2 * ny - (k == 0))], 8 + run)
        re_cols = []
        im_cols = []
        rhs = []
        for y in range(ny):
            p = y * nz + 2 * run
            cols = pl.ds(pl.multiple_of(p * own, 2 * own), 2 * own)
            hot = hot_a[:, cols]
            at = jnp.concatenate([recv1[p], recv1[p + 1]], axis=1)
            re_cols.append(hot * at[0:1, :])
            im_cols.append(hot * at[1:2, :])
            rhs.append(hot_b[:, cols])
        spread = jnp.concatenate(
            [jnp.concatenate(re_cols, axis=1), jnp.concatenate(im_cols, axis=1)], axis=0
        )
        boxed += lax.dot_general(
            spread, jnp.concatenate(rhs, axis=1), NT, preferred_element_type=F32
        )
    boxed = boxed.astype(BF)
    hb = box // 2
    hg = grid // 2

    y_half = [
        jnp.dot(
            jnp.concatenate([boxed[0:box, n * hb : (n + 1) * hb], boxed[box:, n * hb : (n + 1) * hb]], axis=1),
            y_inv[n * box : (n + 1) * box, :],
            preferred_element_type=F32,
        )
        for n in range(2)
    ]
    near = (y_half[0] + y_half[1]).astype(BF)
    over = (y_half[0] - y_half[1]).astype(BF)
    for n in range(2):
        for t in range(2):
            rows = slice(n * box + t * hb, n * box + (t + 1) * hb)
            half[rows, 0:hg] = near[n * hb : (n + 1) * hb, t * hg : (t + 1) * hg]
            half[rows, hg:grid] = over[n * hb : (n + 1) * hb, t * hg : (t + 1) * hg]

    for t in range(2):
        x_half = [
            jnp.dot(
                x_inv[n * grid + t * hg : n * grid + (t + 1) * hg, :],
                half[n * box : (n + 1) * box, :],
                preferred_element_type=F32,
            )
            for n in range(2)
        ]
        one = pot[0, 0:hg, :].astype(F32) * (x_half[0] + x_half[1])
        two = pot[0, hg:grid, :].astype(F32) * (x_half[0] - x_half[1])
        prod[t * hg : (t + 1) * hg, :] = (one + two).astype(BF)
        prod[grid + t * hg : grid + (t + 1) * hg, :] = (one - two).astype(BF)

    plus = []
    minus = []
    for n in range(2):
        hf = jnp.dot(
            fwd[n * box : (n + 1) * box, :],
            prod[n * grid : (n + 1) * grid, :],
            preferred_element_type=F32,
        )
        add = (hf[:, 0:hg] + hf[:, hg:grid]).astype(BF)
        sub = (hf[:, 0:hg] - hf[:, hg:grid]).astype(BF)
        plus.append(jnp.concatenate([add[0:hb], add[hb:box]], axis=1))
        minus.append(jnp.concatenate([sub[0:hb], sub[hb:box]], axis=1))

    def pass_on():
        arrived(gath.at[0], 1)

        @pl.when(zhi == 0)
        def _():
            forward(me_b, partner, 1)

        for peer in x_peers:
            forward(partner, peer, 3)

    @pl.when(zhi == 0)
    def _():
        pass_on()

    cells = [
        lax.dot_general(
            fwd[n * box : (n + 1) * box, :],
            jnp.concatenate(side, axis=0),
            NT,
            preferred_element_type=F32,
        ).astype(BF)
        for n, side in enumerate((plus, minus))
    ]
    cell = jnp.concatenate(
        [cells[0][0:hb], cells[1][0:hb], cells[0][hb:box], cells[1][hb:box]], axis=0
    )

    width = 2 * own
    for k in range(runs):
        run = low * (runs - 1 - k) + (1 - low) * k
        for dy in y_far:
            p = place_of(dy, 2 * run)
            cols = pl.ds(pl.multiple_of(p * own, width), width)
            picked = jnp.dot(cell, hot_a[:, cols], preferred_element_type=F32)
            hot = hot_b[:, cols].astype(F32)
            re = jnp.sum(picked[0:box] * hot, axis=0, keepdims=True)
            im = jnp.sum(picked[box : 2 * box] * hot, axis=0, keepdims=True)
            both = jnp.concatenate([re, im], axis=0).astype(BF)
            for q in range(2):
                send2[p + q] = both[:, q * own : (q + 1) * own]
        for dy in y_far:
            for q in range(2):
                peer = place_of(dy, 2 * run + q)

                def push(peer=peer):
                    send(send2.at[peer], recv2.at[me_p], 2, 12 + mine, {"pw": peer})

                if dy:
                    push()
                else:
                    pl.when(peer != me_p)(push)
    recv2[me_p] = send2[me_p]

    arrived(gath.at[0], 0)

    @pl.when(core == 0)
    def _():
        forward(me_b, sibling, 0)

    arrived(gath.at[pl.ds(0, len(x_peers))], 2)
    for peer in x_peers:
        forward(peer, sibling, 4)
    @pl.when(zhi == 1)
    def _():
        pass_on()

    forward(partner, sibling, 4)
    arrived(gath.at[pl.ds(0, len(x_peers))], 3)
    for peer in x_peers:
        forward(peer + 2 - 4 * zhi, sibling, 4)

    arrived(gath.at[pl.ds(0, bands // 2 - 1)], 4)

    span = 4 * ny
    even = lax.rem(lax.broadcasted_iota(jnp.int32, (span, own), 0), 2) == 0
    re_sum = [jnp.zeros((8, own), F32)] * bands
    im_sum = [jnp.zeros((8, own), F32)] * bands
    for k, run in enumerate(nearest):
        arrived(recv2.at[pl.ds(0, 2 * ny - (k == 0))], 12 + run)
        got = [recv2[y * nz + 2 * run + q].astype(F32) for y in range(ny) for q in range(2)]
        here = jnp.concatenate(got, axis=0)
        turned = jnp.where(
            even, pltpu.roll(here, span - 1, axis=0), -pltpu.roll(here, 1, axis=0)
        )
        rows = pl.ds(pl.multiple_of(run * span, span), span)
        back[rows, :] = here.astype(BF)
        for i in range(bands):
            other = gath[i, rows, :].astype(F32)
            by_re = other * here
            by_im = other * turned
            for t in range(0, span, 8):
                re_sum[i] = re_sum[i] + by_re[t : t + 8]
                im_sum[i] = im_sum[i] + by_im[t : t + 8]
    scale = math.sqrt(box / slab) / math.sqrt(planes * own * box)
    lanes = jnp.concatenate(
        [jnp.sum(t, axis=0, keepdims=True) for t in re_sum + im_sum], axis=0
    )
    total = jnp.sum(lanes, axis=1, keepdims=True) * scale
    on_lane = lax.broadcasted_iota(jnp.int32, (2 * bands, own), 0) == lax.broadcasted_iota(
        jnp.int32, (2 * bands, own), 1
    )
    part[...] = jnp.sum(jnp.where(on_lane, total, 0.0), axis=0, keepdims=True)
    exchange(lambda peer: part, parts, 3, 7)
    parts[me_p] = part[...]

    out = lax.dot_general(back[...], z_fwd[...], TN, preferred_element_type=F32)
    applied_ref[0, 0] = jnp.where(inside, out[:, 0:box], 0.0).astype(BF)
    applied_ref[0, 1] = jnp.where(inside, out[:, box : 2 * box], 0.0).astype(BF)

    arrived(parts.at[pl.ds(0, planes - 1)], 7)
    summed = jnp.sum(parts[...], axis=0)
    corr_ref[0] = summed[:, 0:bands]
    corr_ref[1] = summed[:, bands : 2 * bands]

    for sem, ref in (
        (0, gath.at[pl.ds(0, bands - 1)]),
        (1, recv1.at[pl.ds(0, planes - 1)]),
        (2, recv2.at[pl.ds(0, planes - 1)]),
        (3, parts.at[pl.ds(0, planes - 1)]),
    ):
        pltpu.make_async_copy(ref, ref, send_sem.at[sem]).wait()


def local(band_coeffs, potential, stick_list):
    bands = lax.axis_size("band")
    planes = lax.axis_size("pw")
    own = band_coeffs.shape[2]
    box = band_coeffs.shape[3]
    grid = potential.shape[1]
    slab = potential.shape[0] * planes
    z_inv, z_fwd, y_inv, x_inv, fwd = (jnp.asarray(t) for t in make_tables(box, grid, slab))
    sticks = stick_list.T.reshape(2, planes, own).transpose(1, 0, 2)
    any_space = pl.BlockSpec(memory_space=pl.ANY)
    vmem = pl.BlockSpec(memory_space=pltpu.VMEM)
    applied, corr = pl.pallas_call(
        functools.partial(kernel, (bands, planes, box, grid, own, slab)),
        out_shape=(
            pltpu.VMEM(band_coeffs.shape, BF),
            pltpu.VMEM((2, 1, bands), F32),
        ),
        in_specs=[any_space] * 8,
        out_specs=(vmem, vmem),
        scratch_shapes=[
            pltpu.VMEM(band_coeffs.shape, BF),
            pltpu.VMEM(potential.shape, BF),
            pltpu.VMEM(sticks.shape, jnp.int32),
            pltpu.VMEM(z_inv.shape, BF),
            pltpu.VMEM(z_fwd.shape, BF),
            pltpu.VMEM(y_inv.shape, BF),
            pltpu.VMEM(x_inv.shape, BF),
            pltpu.VMEM(fwd.shape, BF),
            pltpu.VMEM((box, planes * own), BF),
            pltpu.VMEM((box, planes * own), BF),
            pltpu.VMEM((2 * box, grid), BF),
            pltpu.VMEM((2 * grid, grid), BF),
            pltpu.VMEM((slab, 2, own), BF),
            pltpu.VMEM((planes, 2, own), BF),
            pltpu.VMEM((planes, 2, own), BF),
            pltpu.VMEM((slab, 2, own), BF),
            pltpu.VMEM((2 * slab, own), BF),
            pltpu.VMEM((bands, 2 * slab, own), BF),
            pltpu.VMEM((1, own), F32),
            pltpu.VMEM((planes, 1, own), F32),
            pltpu.SemaphoreType.DMA((8,)),
            pltpu.SemaphoreType.DMA((4,)),
            pltpu.SemaphoreType.DMA((16,)),
        ],
        compiler_params=pltpu.CompilerParams(
            collective_id=0, has_side_effects=True, vmem_limit_bytes=56 * 1024 * 1024
        ),
        name="local_potential",
    )(band_coeffs, potential, sticks, z_inv, z_fwd, y_inv, x_inv, fwd)
    return applied, corr.transpose(0, 2, 1)


def solution(mesh):
    return jax.shard_map(
        local,
        mesh=mesh,
        in_specs=(P("band", None, "pw", None), P("pw", None, None), P()),
        out_specs=(P("band", None, "pw", None), P(None, None, "band")),
        check_vma=False,
    )
```
